32 devices in a mesh: group: 2 (over y), expert: 4 (over z), query: 2 (over x), dp: 2 (over core).
Axes of the slice: x: 2, y: 2, z: 4, core: 2. Of those that a mesh axis runs over, the one named last changes fastest.
Arguments:
- tokens: bfloat16 [4096, 2048], P(('group', 'expert', 'query', 'dp')), parts along dimension 0, may hold values from -6 to 6
- route_ids: int32 [4096, 4], P(('group', 'expert', 'query', 'dp')), parts along dimension 0, may hold values from 0 to 7, all different within a row; in each aligned block of 128 rows (0 to 127, 128 to 255, ...) at most 128 rows name the same one
- gate_values: float32 [4096, 4], P(('group', 'expert', 'query', 'dp')), parts along dimension 0, may hold values from 0.1 to 1
- passage_lengths: int32 [64], P(('group', 'expert', 'query', 'dp')), parts along dimension 0, may hold values from 16 to 64
- gate_weight: bfloat16 [8, 2048, 384], P(('expert', 'query'), None, 'dp'), may hold values from -0.125 to 0.125
- up_weight: bfloat16 [8, 2048, 384], P(('expert', 'query'), None, 'dp'), may hold values from -0.125 to 0.125
- down_weight: bfloat16 [8, 2048, 384], P(('expert', 'query'), None, 'dp'), may hold values from -0.3125 to 0.3125
- proj_weight: bfloat16 [2048, 128], replicated, may hold values from -0.125 to 0.125
- queries: bfloat16 [128, 32, 128], P(('group', 'query')), parts along dimension 0, may hold values from -0.59765625 to 0.59765625
Outputs:
- scores: float32 [64, 64], P(('group', 'expert', 'query', 'dp')), parts along dimension 0
The draws below stay inside these ranges and needn't reach their ends.
There are 2 independent parts, one for each index of `group`. The reference program is written for one: setup_inputs(seed, part) draws one part's arguments, and reference() takes and returns one part's arrays. A program takes and returns all parts, laid end to end along the dimension named above; an argument that names none is the same for every part. Nothing has to cross between parts.
Inputs may be any that keep to these rules, and one draw needn't show every extreme that they name: `route_ids`: in the rows of one device no expert is named more than 128 times, a bound that some block reaches.
All inputs are finite; a program needn't handle non-finite values.
Results may differ from the reference program's by a relative error of at most 0.0006.
Values may be sent and summed in bfloat16 or wider, within the bound.
A program may use at most 64 MiB of HBM per device.

```python
import math
import jax
import jax.numpy as jnp
import numpy as np
from jax import lax

D = 2048
FF = 384
TOPK = 4
PROJ = 128
QLEN = 32
PLEN = 64
TOK_DEV = 128
EXPERTS = 8
CAP = 128
NPASS = 32
TOKENS = 2048
NQ = 64
N_EXPERT = 4
N_QUERY = 2
N_DP = 2


def touch_ends(values, rng, smallest, top_value):
    shape = values.shape
    index_at = [jax.random.randint(jax.random.fold_in(rng, axis), (), 0, shape[axis]) for axis in range(len(shape))]
    values = values.at[tuple(index_at)].set(smallest)
    longest = shape.index(max(shape))
    index_at[longest] = (index_at[longest] + 1) % shape[longest]
    return values.at[tuple(index_at)].set(top_value)


def block_scale(stream_key, shape, cuts, least, high):
    factor_of = 1.0
    for axis_at, parts in cuts:
        heights = jax.random.uniform(jax.random.fold_in(jax.random.fold_in(stream_key, 6), axis_at), (parts,), jnp.float32, least / len(cuts), high / len(cuts))
        factor_of = factor_of * jnp.repeat(jnp.exp(heights), shape[axis_at] // parts).reshape((-1,) + (1,) * (len(shape) - 1 - axis_at))
    return factor_of


def shared_out(rng, own, number, rows, count, top, reach, skew):
    order = jax.random.permutation(rng, count)
    heavy_load, common = shares(count, rows * top, reach, skew, True), shares(count, rows * top, reach, skew, False)
    places = jnp.arange(count)

    def named(lengths, rotation):
        used = int((lengths > 0).sum())
        fixed = max(1, used // 4)
        moved = fixed + (places - fixed + rotation * (used - fixed)) % max(1, count - fixed)
        return jnp.zeros((count,), jnp.int32).at[order[jnp.where(places < fixed, places, moved)]].set(jnp.asarray(lengths, jnp.int32))

    lengths = jnp.where(number % 4 == 0, named(heavy_load, number // 4), named(common, number - number // 4 - 1))
    mixed = jax.random.permutation(jax.random.fold_in(own, 3), count)
    source_of, taker = mixed[0:count // 2 * 2:2], mixed[1:count // 2 * 2:2]
    slack = jnp.minimum(lengths[source_of] - 1, reach - lengths[taker]) // 2
    slack = jnp.where((source_of == order[0]) | (taker == order[0]) | (lengths[taker] == 0), 0, jnp.maximum(slack, 0))
    moved = jax.random.randint(jax.random.fold_in(own, 4), (count // 2,), 0, 1 << 20) % (slack + 1)
    lengths = lengths.at[source_of].add(-moved).at[taker].add(moved)
    members = jnp.searchsorted(jnp.cumsum(lengths), jnp.arange(rows * top), side="right").astype(jnp.int32)
    grid = members.reshape(top, rows).T
    grid = grid[jax.random.permutation(jax.random.fold_in(own, 1), rows)]
    rotation = jax.random.randint(jax.random.fold_in(own, 2), (rows, 1), 0, top)
    return jnp.take_along_axis(grid, (jnp.arange(top)[None, :] + rotation) % top, axis=1)


def shares(number_of, total, most, skew, full):
    loads = [(1 << 20) // math.isqrt(grade ** skew) + 1 for grade in range(1, number_of + 1)]
    largest = most if full else min(most, max(-(-total // number_of), total * loads[0] // sum(loads)))
    least = 1 if total - largest >= number_of - 1 else 0
    counts, spare = [largest] + [least] * (number_of - 1), total - largest - least * (number_of - 1)
    while spare > 0:
        movable = [i for i in range(1, number_of) if counts[i] < largest] or [i for i in range(1, number_of) if counts[i] < most]
        whole, budget = sum([loads[i] for i in movable]), spare
        for i in movable:
            addition = min(most - counts[i], max(1, budget * loads[i] // whole), spare)
            counts[i] = counts[i] + addition
            spare = spare - addition
    return np.array(counts)


def normal_values(rng, dims, spread, bound, split=(), kind=jnp.bfloat16):
    entries = jax.random.normal(rng, dims, jnp.float32) * spread
    if len(split) > 0:
        entries = block_scale(rng, dims, split, -0.22, 0.18) * entries
    return jnp.clip(entries, min=-bound, max=bound).astype(kind)


def setup_inputs(seed: int = 0, part: int = 0) -> dict:
    arg_keys = jax.random.split(jax.random.key(seed), 10)
    part_splits = jax.random.split(jax.random.fold_in(arg_keys[9], part), 10)
    tokens = normal_values(part_splits[0], (TOKENS, D), 1.0, 6.0, ((0, 16),))
    route_ids_keys = jax.random.split(jax.random.fold_in(part_splits[1], 1), TOKENS // TOK_DEV)
    route_ids_turns = jax.random.permutation(jax.random.fold_in(part_splits[1], 3), TOKENS // TOK_DEV)
    route_ids = jax.vmap(lambda own, number: shared_out(jax.random.fold_in(part_splits[1], 2), own, number, TOK_DEV, EXPERTS, TOPK, CAP, 2))(route_ids_keys, route_ids_turns).reshape((TOKENS, TOPK))
    gate_values = jnp.clip(jnp.exp(math.log(1.0) - 2.3025851 * jax.random.uniform(part_splits[2], (TOKENS, TOPK), jnp.float32) ** block_scale(part_splits[2], (TOKENS, TOPK), ((0, 16),), -0.2, 0.2)), 0.1, 1.0)
    passage_lengths = touch_ends(jax.random.randint(part_splits[3], (NPASS,), PLEN // 4, PLEN + 1), jax.random.fold_in(part_splits[3], 1), PLEN // 4, PLEN).astype(jnp.int32)
    gate_weight = normal_values(arg_keys[4], (EXPERTS, D, FF), D ** -0.5, 0.125, ((0, 8), (2, 2)))
    up_weight = normal_values(arg_keys[5], (EXPERTS, D, FF), D ** -0.5, 0.125, ((0, 8), (2, 2)))
    down_weight = normal_values(arg_keys[6], (EXPERTS, D, FF), FF ** -0.5, 0.3125, ((0, 8), (2, 2)))
    proj_weight = normal_values(arg_keys[7], (D, PROJ), D ** -0.5, 0.125)
    queries = normal_values(part_splits[8], (NQ, QLEN, PROJ), 0.1, 0.59765625, ((0, 2),))
    return dict(tokens=tokens, route_ids=route_ids, gate_values=gate_values, passage_lengths=passage_lengths, gate_weight=gate_weight, up_weight=up_weight, down_weight=down_weight, proj_weight=proj_weight, queries=queries)


def reference(tokens, route_ids, gate_values, passage_lengths, gate_weight, up_weight, down_weight, proj_weight, queries):
    token_count = tokens.shape[0]
    flat_routes = route_ids.reshape(-1)
    assignments = flat_routes.shape[0]
    flat_gates = gate_values.reshape(-1)
    room = N_EXPERT * N_QUERY * N_DP * CAP

    def per_expert(mixed_rows, expert_id):
        row_index = jnp.nonzero(flat_routes == expert_id, size=room, fill_value=assignments)[0]
        token_index = row_index // TOPK
        expert_rows = jnp.take(tokens, token_index, axis=0, mode='fill', fill_value=0)
        gate_act = jnp.dot(expert_rows, gate_weight[expert_id], preferred_element_type=jnp.float32)
        up_act = jnp.dot(expert_rows, up_weight[expert_id], preferred_element_type=jnp.float32)
        hidden = (jax.nn.silu(gate_act) * up_act).astype(jnp.bfloat16)
        expert_out = lax.dot_general(hidden, down_weight[expert_id], (((1,), (1,)), ((), ())), preferred_element_type=jnp.float32).astype(jnp.bfloat16)
        weights = jnp.take(flat_gates, row_index, mode='fill', fill_value=0)
        mixed_rows = mixed_rows.at[token_index].add(expert_out.astype(jnp.float32) * weights[:, None], mode='drop')
        return (mixed_rows, None)
    mixed_rows, _ = lax.scan(per_expert, tokens.astype(jnp.float32), jnp.arange(EXPERTS, dtype=jnp.int32))
    projected = jnp.dot(mixed_rows, proj_weight.astype(jnp.float32), precision=lax.Precision.HIGHEST)
    lengths_norm = jnp.sqrt(lax.optimization_barrier(jnp.sum(projected * projected, axis=-1, keepdims=True)) + 1e-06)
    embedding = (projected / lengths_norm).astype(jnp.bfloat16)
    passages = passage_lengths.shape[0]
    blocks = embedding.reshape(passages, PLEN, PROJ)
    live_mask = jnp.arange(PLEN, dtype=jnp.int32)[None, :] < passage_lengths[:, None]
    query_rows = queries.reshape(-1, PROJ)

    def score_passage(inputs):
        passage_block, passage_live = inputs
        raw_scores = jnp.dot(passage_block, query_rows.T, preferred_element_type=jnp.float32)
        raw_scores = jnp.where(passage_live[:, None], raw_scores, -jnp.inf)
        return lax.optimization_barrier(jnp.sum(lax.optimization_barrier(jnp.max(raw_scores, axis=0)).reshape(-1, QLEN), axis=-1))
    return lax.map(score_passage, (blocks, live_mask))
```

```python
import functools

import jax
import jax.numpy as jnp
from jax import lax
from jax.experimental import pallas as pl
from jax.experimental.pallas import tpu as pltpu
from jax.sharding import PartitionSpec as P

PLEN = 64
MESH = pl.DeviceIdType.MESH
LANES = 128
PIECES = 2
W_PIECES = 2


def when_all(conds, body):
    live = [c for c in conds if c is not None]
    if live:
        pl.when(functools.reduce(jnp.logical_and, live))(body)
    else:
        body()


def dense_kernel(
    n_exp,
    tokens,
    gate,
    up,
    down,
    proj,
    queries,
    routes,
    gates,
    plens,
    out,
    tok,
    gate_v,
    up_v,
    down_v,
    proj_v,
    w_all,
    v_all,
    q_all,
    comb,
    acc,
    ret,
    base,
    local_sem,
    tok_ss,
    tok_rs,
    comb_ss,
    comb_rs,
    own_ss,
    own_rs,
    wx_ss,
    wx_rs,
    wy_ss,
    wy_rs,
    wd_ss,
    wd_rs,
    v_ss,
    v_rs,
    q_ss,
    q_rs,
    ret_ss,
    ret_rs,
):
    z, x = lax.axis_index("expert"), lax.axis_index("query")
    y, c = lax.axis_index("group"), lax.axis_index("dp")
    rows, width = tokens.shape
    units = gate.shape[1]
    full = units // LANES * LANES
    piece = rows // PIECES
    half_rows = width // 2
    w_rows = half_rows // W_PIECES
    top = routes.shape[0]

    loads = [
        pltpu.make_async_copy(gate, gate_v, local_sem.at[0]),
        pltpu.make_async_copy(up, up_v, local_sem.at[1]),
        pltpu.make_async_copy(tokens, tok.at[z], local_sem.at[2]),
        pltpu.make_async_copy(down, down_v, local_sem.at[3]),
        pltpu.make_async_copy(proj, proj_v, local_sem.at[4]),
        pltpu.make_async_copy(queries, q_all.at[x], local_sem.at[5]),
    ]
    for load in loads:
        load.start()

    barrier = pltpu.get_barrier_semaphore()
    partners = [{"expert": lax.rem(z + k, n_exp)} for k in range(1, n_exp)]
    partners += [{"dp": 1 - c}, {"query": 1 - x}, {"group": 1 - y}, {"query": 1 - x, "dp": 1 - c}]
    for who in partners:
        pl.semaphore_signal(barrier, inc=1, device_id=who, device_id_type=MESH)

    row_id = lax.broadcasted_iota(jnp.int32, comb.shape[1:], 0)
    spread = jnp.zeros(comb.shape[1:], jnp.float32)
    for k in range(top):
        spread += jnp.where(routes[k : k + 1, :] == row_id, gates[k : k + 1, :], 0.0)
    comb[z] = spread
    pl.semaphore_wait(barrier, len(partners))

    def remote(src, dst, ss, rs, who):
        return pltpu.make_async_remote_copy(
            src_ref=src, dst_ref=dst, send_sem=ss, recv_sem=rs, device_id=who, device_id_type=MESH
        )

    def tok_copy(step, owner, h, src=None):
        part = pl.ds(h * piece, piece)
        dst = tok.at[owner, part]
        return remote(
            dst if src is None else src.at[part],
            dst,
            tok_ss.at[(step + 1) // 2, owner, h],
            tok_rs.at[owner, h],
            {"expert": jnp.clip(z + step, 0, n_exp - 1)},
        )

    for h in range(PIECES):
        pl.when(z + 1 < n_exp)(lambda h=h: tok_copy(1, z, h, tokens).start())
        pl.when(z > 0)(lambda h=h: tok_copy(-1, z, h, tokens).start())

    def comb_copy(k):
        return remote(
            comb.at[z], comb.at[z], comb_ss.at[k], comb_rs.at[z], {"expert": lax.rem(z + k, n_exp)}
        )

    for k in range(1, n_exp):
        comb_copy(k).start()

    own = 2 * x + c
    other = 2 * (1 - x) + c
    loads[0].wait()
    loads[1].wait()
    block = width // 8

    def arrange(i, _):
        part = pl.ds(i * block, block)
        g, u = gate_v[part, :], up_v[part, :]
        w_all[own, part, :full] = g[:, :full]
        w_all[own, part, full : 2 * full] = u[:, :full]
        w_all[own, part, 2 * full :] = jnp.concatenate([g[:, full:], u[:, full:]], axis=1)
        return 0

    lax.fori_loop(0, 8, arrange, 0)

    def w_part(side, k):
        return pl.ds(side * half_rows + k * w_rows, w_rows)

    def wx_copy(k):
        part = w_part(y, k)
        ref = w_all.at[own, part]
        return remote(ref, ref, wx_ss.at[k], wx_rs.at[k], {"query": 1 - x})

    def wy_copy(k):
        ref = w_all.at[other, w_part(y, k)]
        return remote(ref, ref, wy_ss.at[k], wy_rs.at[k], {"group": 1 - y})

    def wd_copy(from_y, k):
        ref = w_all.at[other, w_part(1 - y if from_y else y, k)]
        return remote(ref, ref, wd_ss.at[from_y, k], wd_rs.at[from_y, k], {"dp": 1 - c})

    own_copy = remote(w_all.at[own], w_all.at[own], own_ss, own_rs, {"dp": 1 - c})

    for k in range(W_PIECES):
        wx_copy(k).start()
    own_copy.start()

    loads[3].wait()
    loads[4].wait()
    folded = lax.dot_general(
        down_v[...], proj_v[...], (((0,), (0,)), ((), ())), preferred_element_type=jnp.float32
    )
    high = folded.astype(jnp.bfloat16)
    low = (folded - high.astype(jnp.float32)).astype(jnp.bfloat16)
    out_width = proj.shape[1]
    pad_rows = v_all.shape[1] - units
    v_all[own, :units, :out_width] = high
    v_all[own, :units, out_width:] = low
    v_all[own, units:, :] = jnp.zeros((pad_rows, 2 * out_width), jnp.bfloat16)

    loads[2].wait()
    base[...] = jnp.dot(tok[z], proj_v[...], preferred_element_type=jnp.float32)

    v_to = [{"dp": 1 - c}, {"query": 1 - x}, {"query": 1 - x, "dp": 1 - c}]
    v_copies = [remote(v_all.at[own], v_all.at[own], v_ss.at[i], v_rs.at[i], who) for i, who in enumerate(v_to)]
    for copy in v_copies:
        copy.start()
    q_copy = remote(queries, q_all.at[x], q_ss, q_rs, {"query": 1 - x})
    q_copy.start()

    def expert_rows(owner, first, count, expert, halves_from):
        rows_in = tok[owner, pl.ds(first, count), :]
        pick = jnp.sum(
            jnp.where(row_id == z * 2 + expert, comb[owner], 0.0), axis=0, keepdims=True
        )
        scale = jnp.broadcast_to(pick, (out_width, rows)).T[first : first + count]

        def one(c_at, total):
            j = 2 * expert + c_at
            act = jnp.dot(rows_in, w_all[j], preferred_element_type=jnp.float32)
            g, u = act[:, :full], act[:, full : 2 * full]
            t = act[:, 2 * full :]
            main = g / (1.0 + jnp.exp(-g)) * u
            last = t / (1.0 + jnp.exp(-t)) * pltpu.roll(t, LANES // 2, 1)
            hidden = jnp.concatenate([main, last], axis=1).astype(jnp.bfloat16)
            both = jnp.dot(hidden, v_all[j], preferred_element_type=jnp.float32)
            return total + (both[:, :out_width] + both[:, out_width:])

        total = lax.fori_loop(0, 2, one, jnp.zeros((count, out_width), jnp.float32))
        return total * scale

    own_copy.wait_recv()
    v_copies[0].wait_recv()
    acc[z] = expert_rows(z, 0, rows, x, 0)

    def take(d, h):
        for side in (-1, 1):
            owner = jnp.clip(z + side * d, 0, n_exp - 1)
            inside = (z - d >= 0) if side < 0 else (z + d < n_exp)

            def arrive(side=side, owner=owner):
                tok_copy(1, owner, h).wait_recv()

                if d < n_exp - 1:
                    onward = (z + 1 < n_exp) if side < 0 else (z > 0)
                    pl.when(onward)(lambda: tok_copy(-side, owner, h).start())

            pl.when(inside)(arrive)

    def comb_wait(k):
        src = lax.rem(z + n_exp - k, n_exp)
        remote(
            comb.at[src], comb.at[src], comb_ss.at[k], comb_rs.at[src], {"expert": src}
        ).wait_recv()

    for k in range(1, n_exp):
        comb_wait(k)

    x_taken = 0

    def take_x(k):
        part = w_part(y, k)
        remote(
            w_all.at[other, part], w_all.at[other, part], wx_ss.at[k], wx_rs.at[k], {"query": 1 - x}
        ).wait_recv()
        wy_copy(k).start()
        wd_copy(0, k).start()

    for d in range(1, n_exp - 1):
        for h in range(PIECES):
            take(d, h)
            if (d > 1 or h == PIECES - 1) and x_taken < W_PIECES:
                take_x(x_taken)
                x_taken += 1

        def near(owner, _, d=d):
            @pl.when(jnp.abs(owner - z) == d)
            def _():
                acc[owner] = expert_rows(owner, 0, rows, x, 0)

            return 0

        lax.fori_loop(0, n_exp, near, 0)
    while x_taken < W_PIECES:
        take_x(x_taken)
        x_taken += 1

    for k in range(W_PIECES):
        part = w_part(1 - y, k)
        ref = w_all.at[other, part]
        remote(ref, ref, wy_ss.at[k], wy_rs.at[k], {"group": 1 - y}).wait_recv()
        wd_copy(1, k).start()
    peer = 2 * (1 - x) + 1 - c
    for from_y in range(2):
        for k in range(W_PIECES):
            ref = w_all.at[peer, w_part(1 - y if from_y else y, k)]
            remote(ref, ref, wd_ss.at[from_y, k], wd_rs.at[from_y, k], {"dp": 1 - c}).wait_recv()
    v_copies[1].wait_recv()
    v_copies[2].wait_recv()

    def far(owner, _):
        @pl.when(jnp.abs(owner - z) < n_exp - 1)
        def _():
            acc[owner] += expert_rows(owner, 0, rows, 1 - x, 0)

        return 0

    lax.fori_loop(0, n_exp, far, 0)

    def ret_copy(owner, h):
        part = pl.ds(h * piece, piece)
        return remote(
            acc.at[owner, part],
            ret.at[z, part],
            ret_ss.at[owner, h],
            ret_rs.at[z, h],
            {"expert": owner},
        )

    def ret_wait(src, h):
        part = pl.ds(h * piece, piece)
        remote(
            acc.at[src, part], ret.at[src, part], ret_ss.at[src, h], ret_rs.at[src, h], {"expert": src}
        ).wait_recv()

    for owner in range(n_exp):
        @pl.when(jnp.logical_and(jnp.abs(owner - z) < n_exp - 1, owner != z))
        def _(owner=owner):
            for h in range(PIECES):
                ret_copy(owner, h).start()

    @pl.when(jnp.logical_or(z == 0, z == n_exp - 1))
    def _():
        owner = n_exp - 1 - z
        for h in range(PIECES):
            tok_copy(1, owner, h).wait_recv()

            def add(e, total, h=h):
                return total + expert_rows(owner, h * piece, piece, e, 0)

            acc[owner, pl.ds(h * piece, piece)] = lax.fori_loop(
                0, 2, add, jnp.zeros((piece, out_width), jnp.float32)
            )
            ret_copy(owner, h).start()

    loads[5].wait()
    q_in = remote(queries, q_all.at[1 - x], q_ss, q_rs, {"query": 1 - x})
    q_in.wait_recv()

    base[...] += acc[z]
    for dist in range(1, n_exp):
        for side in (-1, 1):
            src = z + side * dist
            inside = (src >= 0) if side < 0 else (src < n_exp)

            @pl.when(inside)
            def _(src=jnp.clip(src, 0, n_exp - 1)):
                for h in range(PIECES):
                    ret_wait(src, h)
                base[...] += ret[src]

    projected = base[...]
    norm = jnp.sqrt(jnp.sum(projected * projected, axis=-1, keepdims=True) + 1e-06)
    embedding = (projected / norm).astype(jnp.bfloat16)
    n_pass, n_lab = out.shape
    n_blocks, q_rows = q_all.shape[0], q_all.shape[1]
    q_len = q_rows * n_blocks // n_lab
    token_at = lax.broadcasted_iota(jnp.int32, (PLEN, q_rows), 0)
    label_at = lax.broadcasted_iota(jnp.int32, (q_rows, LANES), 0) // q_len
    column = lax.broadcasted_iota(jnp.int32, (q_rows, LANES), 1)
    total = jnp.zeros((3 * 8, LANES), jnp.float32)
    for b in range(n_blocks):
        raw = lax.dot_general(
            embedding, q_all[b], (((1,), (1,)), ((), ())), preferred_element_type=jnp.float32
        )
        best = [
            jnp.max(
                jnp.where(token_at < plens[p], raw[p * PLEN : (p + 1) * PLEN], -jnp.inf),
                axis=0,
                keepdims=True,
            )
            for p in range(n_pass)
        ]
        best = jnp.concatenate(best + [jnp.zeros((8 - n_pass, q_rows), jnp.float32)], axis=0)
        first = best.astype(jnp.bfloat16).astype(jnp.float32)
        second = (best - first).astype(jnp.bfloat16).astype(jnp.float32)
        third = best - first - second
        parts = jnp.concatenate([first, second, third], axis=0).astype(jnp.bfloat16)
        members = jnp.where(column == label_at + b * (n_lab // n_blocks), 1.0, 0.0).astype(jnp.bfloat16)
        total += jnp.dot(parts, members, preferred_element_type=jnp.float32)
    summed = total[0:8] + total[8:16] + total[16:24]
    out[...] = summed[:n_pass, :n_lab]

    for h in range(PIECES):
        for owner in range(n_exp):
            @pl.when(jnp.logical_and(z + 1 < n_exp, owner <= z))
            def _(owner=owner, h=h):
                tok_copy(1, owner, h).wait_send()

            @pl.when(jnp.logical_and(z > 0, owner >= z))
            def _(owner=owner, h=h):
                tok_copy(-1, owner, h).wait_send()

            @pl.when(owner != z)
            def _(owner=owner, h=h):
                ret_copy(owner, h).wait_send()

    for k in range(1, n_exp):
        comb_copy(k).wait_send()
    for k in range(W_PIECES):
        wx_copy(k).wait_send()
        wy_copy(k).wait_send()
        wd_copy(0, k).wait_send()
        wd_copy(1, k).wait_send()
    own_copy.wait_send()
    for copy in v_copies:
        copy.wait_send()
    q_copy.wait_send()


def dense_on_device(
    n_exp,
    tokens,
    route_ids,
    gate_values,
    passage_lengths,
    gate_weight,
    up_weight,
    down_weight,
    proj_weight,
    queries,
):
    rows, width = tokens.shape
    units = gate_weight.shape[2]
    out_width = proj_weight.shape[1]
    queries2 = queries.reshape(-1, queries.shape[-1])
    n_experts = n_exp * 2
    v_rows = (units // LANES + 1) * LANES
    any_spec = pl.BlockSpec(memory_space=pl.ANY)
    vmem_spec = pl.BlockSpec(memory_space=pltpu.VMEM)
    dma = pltpu.SemaphoreType.DMA
    bf16, f32 = jnp.bfloat16, jnp.float32
    return pl.pallas_call(
        functools.partial(dense_kernel, n_exp),
        out_shape=jax.ShapeDtypeStruct((passage_lengths.shape[0], queries.shape[0] * 2), f32),
        in_specs=[any_spec] * 6 + [vmem_spec] * 2 + [pl.BlockSpec(memory_space=pltpu.SMEM)],
        out_specs=vmem_spec,
        scratch_shapes=[
            pltpu.VMEM((n_exp, rows, width), bf16),
            pltpu.VMEM((width, units), bf16),
            pltpu.VMEM((width, units), bf16),
            pltpu.VMEM((width, units), bf16),
            pltpu.VMEM((width, out_width), bf16),
            pltpu.VMEM((4, width, 2 * units), bf16),
            pltpu.VMEM((4, v_rows, 2 * out_width), bf16),
            pltpu.VMEM((2,) + queries2.shape, bf16),
            pltpu.VMEM((n_exp, n_experts, rows), f32),
            pltpu.VMEM((n_exp, rows, out_width), f32),
            pltpu.VMEM((n_exp, rows, out_width), f32),
            pltpu.VMEM((rows, out_width), f32),
            dma((6,)),
            dma((2, n_exp, PIECES)),
            dma((n_exp, PIECES)),
            dma((n_exp,)),
            dma((n_exp,)),
            dma,
            dma,
            dma((W_PIECES,)),
            dma((W_PIECES,)),
            dma((W_PIECES,)),
            dma((W_PIECES,)),
            dma((2, W_PIECES)),
            dma((2, W_PIECES)),
            dma((3,)),
            dma((3,)),
            dma,
            dma,
            dma((n_exp, PIECES)),
            dma((n_exp, PIECES)),
        ],
        compiler_params=pltpu.CompilerParams(collective_id=0, has_side_effects=True),
    )(
        tokens,
        gate_weight[0],
        up_weight[0],
        down_weight[0],
        proj_weight,
        queries2,
        route_ids.T,
        gate_values.T,
        passage_lengths,
    )


def dense_fits(mesh_shape, rows, units, top):
    experts = mesh_shape["expert"] * mesh_shape["query"]
    pairs = all(mesh_shape[a] == 2 for a in ("group", "query", "dp"))
    capacity = max(2, 2 * rows * top // experts)
    return pairs and mesh_shape["expert"] > 2 and capacity >= rows and units % LANES == LANES // 2


def passage_scores(embedding, live_mask, block_queries):
    query_rows = block_queries.reshape(-1, block_queries.shape[-1])
    raw_scores = jnp.dot(embedding, query_rows.T, preferred_element_type=jnp.float32)
    raw_scores = jnp.where(live_mask[:, None], raw_scores, -jnp.inf)
    best_match = jnp.max(raw_scores.reshape(-1, PLEN, raw_scores.shape[-1]), axis=1)
    return jnp.sum(best_match.reshape(best_match.shape[0], -1, block_queries.shape[1]), axis=-1)


def on_device(
    tokens,
    route_ids,
    gate_values,
    passage_lengths,
    gate_weight,
    up_weight,
    down_weight,
    proj_weight,
    queries,
):
    tok_rows, model_width = tokens.shape
    top_count = route_ids.shape[1]
    experts = lax.axis_size("expert") * lax.axis_size("query")
    capacity = max(2, 2 * tok_rows * top_count // experts)
    assignments = tok_rows * top_count
    flat_routes = route_ids.reshape(-1)
    one_hot = (flat_routes[:, None] == jnp.arange(experts, dtype=jnp.int32)[None, :]).astype(
        jnp.int32
    )
    earlier = jnp.cumsum(one_hot, axis=0) - one_hot
    slot_index = jnp.sum(earlier * one_hot, axis=1)
    slot_target = flat_routes * capacity + slot_index
    slot_owner = (
        jnp.full((experts * capacity,), assignments, jnp.int32)
        .at[slot_target]
        .set(jnp.arange(assignments, dtype=jnp.int32))
    )
    padded = jnp.concatenate([tokens, jnp.zeros((1, model_width), tokens.dtype)], axis=0)
    source_row = jnp.where(slot_owner < assignments, slot_owner // top_count, tok_rows)
    outgoing = padded[source_row].reshape(experts, capacity, model_width)
    arrived = lax.all_to_all(outgoing, ("expert", "query"), split_axis=0, concat_axis=0, tiled=True)
    expert_rows = arrived.reshape(experts * capacity, model_width)
    gate_act = jnp.dot(
        expert_rows,
        lax.all_gather(gate_weight[0], "dp", axis=1, tiled=True),
        preferred_element_type=jnp.float32,
    )
    up_act = jnp.dot(
        expert_rows,
        lax.all_gather(up_weight[0], "dp", axis=1, tiled=True),
        preferred_element_type=jnp.float32,
    )
    hidden = (jax.nn.silu(gate_act) * up_act).astype(jnp.bfloat16)
    accumulated = lax.dot_general(
        hidden,
        lax.all_gather(down_weight[0], "dp", axis=1, tiled=True),
        (((1,), (1,)), ((), ())),
        preferred_element_type=jnp.float32,
    )
    results = accumulated.astype(jnp.bfloat16)
    weights = gate_values.reshape(assignments, 1)
    folded = jnp.dot(results, proj_weight, preferred_element_type=jnp.float32)
    returned_rows = lax.all_to_all(
        folded.reshape(experts, capacity, folded.shape[-1]),
        ("expert", "query"),
        split_axis=0,
        concat_axis=0,
        tiled=True,
    )
    picked = returned_rows.reshape(experts * capacity, folded.shape[-1])[slot_target]
    projected = jnp.dot(tokens, proj_weight, preferred_element_type=jnp.float32) + jnp.sum(
        (picked * weights).reshape(tok_rows, top_count, folded.shape[-1]), axis=1
    )
    lengths_norm = jnp.sqrt(jnp.sum(projected * projected, axis=-1, keepdims=True) + 1e-06)
    embedding = (projected / lengths_norm).astype(jnp.bfloat16)
    position = jnp.arange(tok_rows, dtype=jnp.int32) % PLEN
    live_mask = position < jnp.repeat(passage_lengths, PLEN)
    return passage_scores(
        embedding, live_mask, lax.all_gather(queries, "query", axis=0, tiled=True)
    )


def solution(mesh):
    in_specs = (
        P(("group", "expert", "query", "dp"), None),
        P(("group", "expert", "query", "dp"), None),
        P(("group", "expert", "query", "dp"), None),
        P(("group", "expert", "query", "dp")),
        P(("expert", "query"), None, "dp"),
        P(("expert", "query"), None, "dp"),
        P(("expert", "query"), None, "dp"),
        P(),
        P(("group", "query"), None, None),
    )
    out_specs = P(("group", "expert", "query", "dp"), None)
    sizes = dict(mesh.shape)

    def run(tokens, route_ids, *rest):
        units = rest[2].shape[2]
        if dense_fits(sizes, tokens.shape[0], units, route_ids.shape[1]):
            return dense_on_device(sizes["expert"], tokens, route_ids, *rest)
        return on_device(tokens, route_ids, *rest)

    return jax.shard_map(
        run, mesh=mesh, in_specs=in_specs, out_specs=out_specs, check_vma=False
    )
```

```python
import functools

import jax
import jax.numpy as jnp
from jax import lax
from jax.experimental import pallas as pl
from jax.experimental.pallas import tpu as pltpu
from jax.sharding import PartitionSpec as P

PLEN = 64
MESH = pl.DeviceIdType.MESH
LANES = 128
PIECES = 4
W_PIECES = 4


def dense_kernel(
    n_exp,
    tokens,
    gate,
    up,
    down,
    proj,
    queries,
    routes,
    gates,
    plens,
    out,
    tok,
    down_v,
    proj_v,
    w_all,
    v_all,
    q_all,
    comb,
    acc,
    ret,
    base,
    part_act,
    members,
    local_sem,
    tok_ss,
    tok_rs,
    comb_ss,
    comb_rs,
    own_ss,
    own_rs,
    wx_ss,
    wx_rs,
    wy_ss,
    wy_rs,
    wd_ss,
    wd_rs,
    v_ss,
    v_rs,
    q_ss,
    q_rs,
    ret_ss,
    ret_rs,
):
    z, x = lax.axis_index("expert"), lax.axis_index("query")
    y, c = lax.axis_index("group"), lax.axis_index("dp")
    rows, width = tokens.shape
    units = gate.shape[0]
    full = units // LANES * LANES
    piece = width // PIECES
    half_rows = units
    w_rows = half_rows // W_PIECES
    own = 2 * x + c
    other = 2 * (1 - x) + c
    ends = 2 * full + units - full
    top = routes.shape[0]

    w_own = w_all.at[own]
    arranged = [
        (gate.at[:full], w_own.at[:full]),
        (up.at[:full], w_own.at[full : 2 * full]),
        (gate.at[full:], w_own.at[2 * full : ends]),
        (up.at[full:], w_own.at[ends:]),
        (tokens, tok.at[z]),
        (down, down_v),
        (proj, proj_v),
        (queries, q_all.at[x]),
    ]
    loads = [
        pltpu.make_async_copy(src, dst, local_sem.at[i]) for i, (src, dst) in enumerate(arranged)
    ]
    for load in loads:
        load.start()

    barrier = pltpu.get_barrier_semaphore()
    partners = [{"expert": lax.rem(z + k, n_exp)} for k in range(1, n_exp)]
    partners += [{"dp": 1 - c}, {"query": 1 - x}, {"group": 1 - y}, {"query": 1 - x, "dp": 1 - c}]
    for who in partners:
        pl.semaphore_signal(barrier, inc=1, device_id=who, device_id_type=MESH)

    row_id = lax.broadcasted_iota(jnp.int32, comb.shape[1:], 0)
    spread = jnp.zeros(comb.shape[1:], jnp.float32)
    for k in range(top):
        spread += jnp.where(routes[k : k + 1, :] == row_id, gates[k : k + 1, :], 0.0)
    comb[z] = spread
    pl.semaphore_wait(barrier, len(partners))

    def remote(src, dst, ss, rs, who):
        return pltpu.make_async_remote_copy(
            src_ref=src, dst_ref=dst, send_sem=ss, recv_sem=rs, device_id=who, device_id_type=MESH
        )

    def tok_copy(step, owner, h, src=None):
        part = pl.ds(h * piece, piece)
        dst = tok.at[owner, :, part]
        return remote(
            dst if src is None else src.at[:, part],
            dst,
            tok_ss.at[(step + 1) // 2, owner, h],
            tok_rs.at[owner, h],
            {"expert": jnp.clip(z + step, 0, n_exp - 1)},
        )

    for h in range(PIECES):
        pl.when(z + 1 < n_exp)(lambda h=h: tok_copy(1, z, h, tokens).start())
        pl.when(z > 0)(lambda h=h: tok_copy(-1, z, h, tokens).start())

    def comb_copy(k):
        return remote(
            comb.at[z], comb.at[z], comb_ss.at[k], comb_rs.at[z], {"expert": lax.rem(z + k, n_exp)}
        )

    for k in range(1, n_exp):
        comb_copy(k).start()

    for i in range(4):
        loads[i].wait()

    def w_part(side, k):
        return pl.ds(side * half_rows + k * w_rows, w_rows)

    def wx_copy(k):
        part = w_part(y, k)
        ref = w_all.at[own, part]
        return remote(ref, ref, wx_ss.at[k], wx_rs.at[k], {"query": 1 - x})

    def wy_copy(k):
        ref = w_all.at[other, w_part(y, k)]
        return remote(ref, ref, wy_ss.at[k], wy_rs.at[k], {"group": 1 - y})

    def wd_copy(from_y, k):
        ref = w_all.at[other, w_part(1 - y if from_y else y, k)]
        return remote(ref, ref, wd_ss.at[from_y, k], wd_rs.at[from_y, k], {"dp": 1 - c})

    own_copy = remote(w_all.at[own], w_all.at[own], own_ss, own_rs, {"dp": 1 - c})

    for k in range(W_PIECES):
        wx_copy(k).start()
    own_copy.start()

    loads[5].wait()
    loads[6].wait()
    folded = jnp.dot(down_v[...], proj_v[...], preferred_element_type=jnp.float32)
    high = folded.astype(jnp.bfloat16)
    low = (folded - high.astype(jnp.float32)).astype(jnp.bfloat16)
    out_width = proj.shape[1]
    pad_rows = v_all.shape[1] - units
    v_all[own, :units, :out_width] = high
    v_all[own, :units, out_width:] = low
    v_all[own, units:, :] = jnp.zeros((pad_rows, 2 * out_width), jnp.bfloat16)

    loads[4].wait()
    base[...] = jnp.dot(tok[z], proj_v[...], preferred_element_type=jnp.float32)

    v_to = [{"dp": 1 - c}, {"query": 1 - x}, {"query": 1 - x, "dp": 1 - c}]
    v_copies = [remote(v_all.at[own], v_all.at[own], v_ss.at[i], v_rs.at[i], who) for i, who in enumerate(v_to)]
    for copy in v_copies:
        copy.start()
    q_copy = remote(queries, q_all.at[x], q_ss, q_rs, {"query": 1 - x})
    q_copy.start()

    def product(owner, j, first, count):
        return lax.dot_general(
            tok[owner, :, first : first + count],
            w_all[j, :, first : first + count],
            (((1,), (1,)), ((), ())),
            preferred_element_type=jnp.float32,
        )

    def after(act, j):
        g, u = act[:, :full], act[:, full : 2 * full]
        t = act[:, 2 * full :]
        main = g / (1.0 + jnp.exp(-g)) * u
        last = t / (1.0 + jnp.exp(-t)) * pltpu.roll(t, LANES // 2, 1)
        hidden = jnp.concatenate([main, last], axis=1).astype(jnp.bfloat16)
        both = jnp.dot(hidden, v_all[j], preferred_element_type=jnp.float32)
        return both[:, :out_width] + both[:, out_width:]

    def scale_of(owner, expert):
        pick = jnp.sum(
            jnp.where(row_id == z * 2 + expert, comb[owner], 0.0), axis=0, keepdims=True
        )
        return jnp.broadcast_to(pick, (out_width, rows)).T

    def expert_rows(owner, expert):
        def one(c_at, total):
            j = 2 * expert + c_at
            return total + after(product(owner, j, 0, width), j)

        total = lax.fori_loop(0, 2, one, jnp.zeros((rows, out_width), jnp.float32))
        return total * scale_of(owner, expert)

    own_copy.wait_recv()
    v_copies[0].wait_recv()
    acc[z] = expert_rows(z, x)

    def take(d, h):
        for side in (-1, 1):
            owner = jnp.clip(z + side * d, 0, n_exp - 1)
            inside = (z - d >= 0) if side < 0 else (z + d < n_exp)

            def arrive(side=side, owner=owner):
                tok_copy(1, owner, h).wait_recv()

                if d < n_exp - 1:
                    onward = (z + 1 < n_exp) if side < 0 else (z > 0)
                    pl.when(onward)(lambda: tok_copy(-side, owner, h).start())

            pl.when(inside)(arrive)

    def comb_wait(k):
        src = lax.rem(z + n_exp - k, n_exp)
        remote(
            comb.at[src], comb.at[src], comb_ss.at[k], comb_rs.at[src], {"expert": src}
        ).wait_recv()

    for k in range(1, n_exp):
        comb_wait(k)

    x_taken = 0

    def take_x(k):
        part = w_part(y, k)
        remote(
            w_all.at[other, part], w_all.at[other, part], wx_ss.at[k], wx_rs.at[k], {"query": 1 - x}
        ).wait_recv()
        wy_copy(k).start()
        wd_copy(0, k).start()

    for d in range(1, n_exp - 1):
        for h in range(PIECES):
            take(d, h)
            if h % 2 == (1 if d == 1 else 0) and x_taken < W_PIECES:
                take_x(x_taken)
                x_taken += 1

        def near(owner, _, d=d):
            @pl.when(jnp.abs(owner - z) == d)
            def _():
                acc[owner] = expert_rows(owner, x)

            return 0

        lax.fori_loop(0, n_exp, near, 0)
    while x_taken < W_PIECES:
        take_x(x_taken)
        x_taken += 1

    for k in range(W_PIECES):
        part = w_part(1 - y, k)
        ref = w_all.at[other, part]
        remote(ref, ref, wy_ss.at[k], wy_rs.at[k], {"group": 1 - y}).wait_recv()
        wd_copy(1, k).start()
    peer = 2 * (1 - x) + 1 - c
    for from_y in range(2):
        for k in range(W_PIECES):
            ref = w_all.at[peer, w_part(1 - y if from_y else y, k)]
            remote(ref, ref, wd_ss.at[from_y, k], wd_rs.at[from_y, k], {"dp": 1 - c}).wait_recv()
    v_copies[1].wait_recv()
    v_copies[2].wait_recv()

    def far(owner, _):
        @pl.when(jnp.abs(owner - z) < n_exp - 1)
        def _():
            acc[owner] += expert_rows(owner, 1 - x)

        return 0

    lax.fori_loop(0, n_exp, far, 0)

    def ret_copy(owner):
        return remote(
            acc.at[owner], ret.at[z], ret_ss.at[owner], ret_rs.at[z], {"expert": owner}
        )

    def ret_wait(src):
        remote(
            acc.at[src], ret.at[src], ret_ss.at[src], ret_rs.at[src], {"expert": src}
        ).wait_recv()

    for owner in range(n_exp):
        @pl.when(jnp.logical_and(jnp.abs(owner - z) < n_exp - 1, owner != z))
        def _(owner=owner):
            ret_copy(owner).start()

    n_pass, n_lab = out.shape
    n_blocks, q_rows = q_all.shape[0], q_all.shape[1]
    q_len = q_rows * n_blocks // n_lab
    label_at = lax.broadcasted_iota(jnp.int32, (q_rows, LANES), 0) // q_len
    column = lax.broadcasted_iota(jnp.int32, (q_rows, LANES), 1)
    for b in range(n_blocks):
        members[b] = jnp.where(column == label_at + b * (n_lab // n_blocks), 1.0, 0.0).astype(
            jnp.bfloat16
        )
    base[...] += acc[z]

    @pl.when(jnp.logical_or(z == 0, z == n_exp - 1))
    def _():
        owner = n_exp - 1 - z
        scales = [scale_of(owner, e) for e in range(2)]
        for h in range(PIECES):
            tok_copy(1, owner, h).wait_recv()
            if h < PIECES - 1:

                def more(j, _, h=h):
                    term = product(owner, j, h * piece, piece)
                    part_act[j] = term if h == 0 else part_act[j] + term
                    return 0

                lax.fori_loop(0, 4, more, 0)
        total = None
        for e in range(2):
            term = None
            for c_at in range(2):
                j = 2 * e + c_at
                act = part_act[j] + product(owner, j, width - piece, piece)
                term = after(act, j) if term is None else term + after(act, j)
            total = term * scales[e] if total is None else total + term * scales[e]
        acc[owner] = total
        ret_copy(owner).start()

    loads[7].wait()
    q_in = remote(queries, q_all.at[1 - x], q_ss, q_rs, {"query": 1 - x})
    q_in.wait_recv()

    for dist in range(1, n_exp):
        for side in (-1, 1):
            src = z + side * dist
            inside = (src >= 0) if side < 0 else (src < n_exp)

            @pl.when(inside)
            def _(src=jnp.clip(src, 0, n_exp - 1)):
                ret_wait(src)
                base[...] += ret[src]

    projected = base[...]
    norm = jnp.sqrt(jnp.sum(projected * projected, axis=-1, keepdims=True) + 1e-06)
    scaled = projected / norm
    token_at = lax.broadcasted_iota(jnp.int32, (PLEN, out_width), 0)
    live = []
    for p in range(n_pass):
        block = scaled[p * PLEN : (p + 1) * PLEN]
        live.append(jnp.where(token_at < plens[p], block, block[0:1]))
    embedding = jnp.concatenate(live, axis=0).astype(jnp.bfloat16)
    total = jnp.zeros((3 * 8, LANES), jnp.float32)
    for b in range(n_blocks):
        raw = lax.dot_general(
            embedding, q_all[b], (((1,), (1,)), ((), ())), preferred_element_type=jnp.float32
        )
        best = [
            jnp.max(raw[p * PLEN : (p + 1) * PLEN], axis=0, keepdims=True) for p in range(n_pass)
        ]
        best = jnp.concatenate(best + [jnp.zeros((8 - n_pass, q_rows), jnp.float32)], axis=0)
        first = best.astype(jnp.bfloat16).astype(jnp.float32)
        second = (best - first).astype(jnp.bfloat16).astype(jnp.float32)
        third = best - first - second
        parts = jnp.concatenate([first, second, third], axis=0).astype(jnp.bfloat16)
        total += jnp.dot(parts, members[b], preferred_element_type=jnp.float32)
    summed = total[0:8] + total[8:16] + total[16:24]
    out[...] = summed[:n_pass, :n_lab]

    for h in range(PIECES):
        for owner in range(n_exp):
            @pl.when(jnp.logical_and(z + 1 < n_exp, owner <= z))
            def _(owner=owner, h=h):
                tok_copy(1, owner, h).wait_send()

            @pl.when(jnp.logical_and(z > 0, owner >= z))
            def _(owner=owner, h=h):
                tok_copy(-1, owner, h).wait_send()

    for owner in range(n_exp):
        @pl.when(owner != z)
        def _(owner=owner):
            ret_copy(owner).wait_send()

    for k in range(1, n_exp):
        comb_copy(k).wait_send()
    for k in range(W_PIECES):
        wx_copy(k).wait_send()
        wy_copy(k).wait_send()
        wd_copy(0, k).wait_send()
        wd_copy(1, k).wait_send()
    own_copy.wait_send()
    for copy in v_copies:
        copy.wait_send()
    q_copy.wait_send()


def dense_on_device(
    n_exp,
    tokens,
    route_ids,
    gate_values,
    passage_lengths,
    gate_weight,
    up_weight,
    down_weight,
    proj_weight,
    queries,
):
    rows, width = tokens.shape
    units = gate_weight.shape[2]
    out_width = proj_weight.shape[1]
    queries2 = queries.reshape(-1, queries.shape[-1])
    n_experts = n_exp * 2
    v_rows = (units // LANES + 1) * LANES
    any_spec = pl.BlockSpec(memory_space=pl.ANY)
    vmem_spec = pl.BlockSpec(memory_space=pltpu.VMEM)
    dma = pltpu.SemaphoreType.DMA
    bf16, f32 = jnp.bfloat16, jnp.float32
    return pl.pallas_call(
        functools.partial(dense_kernel, n_exp),
        out_shape=jax.ShapeDtypeStruct((passage_lengths.shape[0], queries.shape[0] * 2), f32),
        in_specs=[any_spec] * 6 + [vmem_spec] * 2 + [pl.BlockSpec(memory_space=pltpu.SMEM)],
        out_specs=vmem_spec,
        scratch_shapes=[
            pltpu.VMEM((n_exp, rows, width), bf16),
            pltpu.VMEM((units, width), bf16),
            pltpu.VMEM((width, out_width), bf16),
            pltpu.VMEM((4, 2 * units, width), bf16),
            pltpu.VMEM((4, v_rows, 2 * out_width), bf16),
            pltpu.VMEM((2,) + queries2.shape, bf16),
            pltpu.VMEM((n_exp, n_experts, rows), f32),
            pltpu.VMEM((n_exp, rows, out_width), f32),
            pltpu.VMEM((n_exp, rows, out_width), f32),
            pltpu.VMEM((rows, out_width), f32),
            pltpu.VMEM((4, rows, 2 * units), f32),
            pltpu.VMEM((2, queries2.shape[0], LANES), bf16),
            dma((8,)),
            dma((2, n_exp, PIECES)),
            dma((n_exp, PIECES)),
            dma((n_exp,)),
            dma((n_exp,)),
            dma,
            dma,
            dma((W_PIECES,)),
            dma((W_PIECES,)),
            dma((W_PIECES,)),
            dma((W_PIECES,)),
            dma((2, W_PIECES)),
            dma((2, W_PIECES)),
            dma((3,)),
            dma((3,)),
            dma,
            dma,
            dma((n_exp,)),
            dma((n_exp,)),
        ],
        compiler_params=pltpu.CompilerParams(collective_id=0, has_side_effects=True),
    )(
        tokens,
        gate_weight[0].T,
        up_weight[0].T,
        down_weight[0].T,
        proj_weight,
        queries2,
        route_ids.T,
        gate_values.T,
        passage_lengths,
    )


def dense_fits(mesh_shape, rows, units, top):
    experts = mesh_shape["expert"] * mesh_shape["query"]
    pairs = all(mesh_shape[a] == 2 for a in ("group", "query", "dp"))
    capacity = max(2, 2 * rows * top // experts)
    return pairs and mesh_shape["expert"] > 2 and capacity >= rows and units % LANES == LANES // 2


def passage_scores(embedding, live_mask, block_queries):
    query_rows = block_queries.reshape(-1, block_queries.shape[-1])
    raw_scores = jnp.dot(embedding, query_rows.T, preferred_element_type=jnp.float32)
    raw_scores = jnp.where(live_mask[:, None], raw_scores, -jnp.inf)
    best_match = jnp.max(raw_scores.reshape(-1, PLEN, raw_scores.shape[-1]), axis=1)
    return jnp.sum(best_match.reshape(best_match.shape[0], -1, block_queries.shape[1]), axis=-1)


def on_device(
    tokens,
    route_ids,
    gate_values,
    passage_lengths,
    gate_weight,
    up_weight,
    down_weight,
    proj_weight,
    queries,
):
    tok_rows, model_width = tokens.shape
    top_count = route_ids.shape[1]
    experts = lax.axis_size("expert") * lax.axis_size("query")
    capacity = max(2, 2 * tok_rows * top_count // experts)
    assignments = tok_rows * top_count
    flat_routes = route_ids.reshape(-1)
    one_hot = (flat_routes[:, None] == jnp.arange(experts, dtype=jnp.int32)[None, :]).astype(
        jnp.int32
    )
    earlier = jnp.cumsum(one_hot, axis=0) - one_hot
    slot_index = jnp.sum(earlier * one_hot, axis=1)
    slot_target = flat_routes * capacity + slot_index
    slot_owner = (
        jnp.full((experts * capacity,), assignments, jnp.int32)
        .at[slot_target]
        .set(jnp.arange(assignments, dtype=jnp.int32))
    )
    padded = jnp.concatenate([tokens, jnp.zeros((1, model_width), tokens.dtype)], axis=0)
    source_row = jnp.where(slot_owner < assignments, slot_owner // top_count, tok_rows)
    outgoing = padded[source_row].reshape(experts, capacity, model_width)
    arrived = lax.all_to_all(outgoing, ("expert", "query"), split_axis=0, concat_axis=0, tiled=True)
    expert_rows = arrived.reshape(experts * capacity, model_width)
    gate_act = jnp.dot(
        expert_rows,
        lax.all_gather(gate_weight[0], "dp", axis=1, tiled=True),
        preferred_element_type=jnp.float32,
    )
    up_act = jnp.dot(
        expert_rows,
        lax.all_gather(up_weight[0], "dp", axis=1, tiled=True),
        preferred_element_type=jnp.float32,
    )
    hidden = (jax.nn.silu(gate_act) * up_act).astype(jnp.bfloat16)
    accumulated = lax.dot_general(
        hidden,
        lax.all_gather(down_weight[0], "dp", axis=1, tiled=True),
        (((1,), (1,)), ((), ())),
        preferred_element_type=jnp.float32,
    )
    results = accumulated.astype(jnp.bfloat16)
    weights = gate_values.reshape(assignments, 1)
    folded = jnp.dot(results, proj_weight, preferred_element_type=jnp.float32)
    returned_rows = lax.all_to_all(
        folded.reshape(experts, capacity, folded.shape[-1]),
        ("expert", "query"),
        split_axis=0,
        concat_axis=0,
        tiled=True,
    )
    picked = returned_rows.reshape(experts * capacity, folded.shape[-1])[slot_target]
    projected = jnp.dot(tokens, proj_weight, preferred_element_type=jnp.float32) + jnp.sum(
        (picked * weights).reshape(tok_rows, top_count, folded.shape[-1]), axis=1
    )
    lengths_norm = jnp.sqrt(jnp.sum(projected * projected, axis=-1, keepdims=True) + 1e-06)
    embedding = (projected / lengths_norm).astype(jnp.bfloat16)
    position = jnp.arange(tok_rows, dtype=jnp.int32) % PLEN
    live_mask = position < jnp.repeat(passage_lengths, PLEN)
    return passage_scores(
        embedding, live_mask, lax.all_gather(queries, "query", axis=0, tiled=True)
    )


def solution(mesh):
    in_specs = (
        P(("group", "expert", "query", "dp"), None),
        P(("group", "expert", "query", "dp"), None),
        P(("group", "expert", "query", "dp"), None),
        P(("group", "expert", "query", "dp")),
        P(("expert", "query"), None, "dp"),
        P(("expert", "query"), None, "dp"),
        P(("expert", "query"), None, "dp"),
        P(),
        P(("group", "query"), None, None),
    )
    out_specs = P(("group", "expert", "query", "dp"), None)
    sizes = dict(mesh.shape)

    def run(tokens, route_ids, *rest):
        units = rest[2].shape[2]
        if dense_fits(sizes, tokens.shape[0], units, route_ids.shape[1]):
            return dense_on_device(sizes["expert"], tokens, route_ids, *rest)
        return on_device(tokens, route_ids, *rest)

    return jax.shard_map(
        run, mesh=mesh, in_specs=in_specs, out_specs=out_specs, check_vma=False
    )
```

```python
import functools

import jax
import jax.numpy as jnp
from jax import lax
from jax.experimental import pallas as pl
from jax.experimental.pallas import tpu as pltpu
from jax.sharding import PartitionSpec as P

PLEN = 64
MESH = pl.DeviceIdType.MESH
LANES = 128
PIECES = 4
W_PIECES = 4


def dense_kernel(
    n_exp,
    tokens,
    gate,
    up,
    down,
    proj,
    queries,
    routes,
    gates,
    plens,
    out,
    tok,
    down_v,
    proj_v,
    w_all,
    v_all,
    q_all,
    comb,
    acc,
    ret,
    base,
    part_act,
    members,
    local_sem,
    tok_ss,
    tok_rs,
    comb_ss,
    comb_rs,
    own_ss,
    own_rs,
    wx_ss,
    wx_rs,
    wy_ss,
    wy_rs,
    wd_ss,
    wd_rs,
    v_ss,
    v_rs,
    q_ss,
    q_rs,
    ret_ss,
    ret_rs,
):
    z, x = lax.axis_index("expert"), lax.axis_index("query")
    y, c = lax.axis_index("group"), lax.axis_index("dp")
    rows, width = tokens.shape
    units = gate.shape[0]
    full = units // LANES * LANES
    piece = width // PIECES
    half_rows = units
    w_rows = half_rows // W_PIECES
    own = 2 * x + c
    other = 2 * (1 - x) + c
    ends = 2 * full + units - full
    top = routes.shape[0]

    w_own = w_all.at[own]
    arranged = [
        (gate.at[:full], w_own.at[:full]),
        (up.at[:full], w_own.at[full : 2 * full]),
        (gate.at[full:], w_own.at[2 * full : ends]),
        (up.at[full:], w_own.at[ends:]),
        (tokens, tok.at[z]),
        (down, down_v),
        (proj, proj_v),
        (queries, q_all.at[x]),
    ]
    loads = [
        pltpu.make_async_copy(src, dst, local_sem.at[i]) for i, (src, dst) in enumerate(arranged)
    ]
    for load in loads:
        load.start()

    barrier = pltpu.get_barrier_semaphore()
    partners = [{"expert": lax.rem(z + k, n_exp)} for k in range(1, n_exp)]
    partners += [{"dp": 1 - c}, {"query": 1 - x}, {"group": 1 - y}]
    for who in partners:
        pl.semaphore_signal(barrier, inc=1, device_id=who, device_id_type=MESH)

    row_id = lax.broadcasted_iota(jnp.int32, comb.shape[1:], 0)
    spread = jnp.zeros(comb.shape[1:], jnp.float32)
    for k in range(top):
        spread += jnp.where(routes[k : k + 1, :] == row_id, gates[k : k + 1, :], 0.0)
    comb[z] = spread
    pl.semaphore_wait(barrier, len(partners))

    def remote(src, dst, ss, rs, who):
        return pltpu.make_async_remote_copy(
            src_ref=src, dst_ref=dst, send_sem=ss, recv_sem=rs, device_id=who, device_id_type=MESH
        )

    def tok_copy(step, owner, h, src=None):
        part = pl.ds(h * piece, piece)
        dst = tok.at[owner, :, part]
        return remote(
            dst if src is None else src.at[:, part],
            dst,
            tok_ss.at[(step + 1) // 2, owner, h],
            tok_rs.at[owner, h],
            {"expert": jnp.clip(z + step, 0, n_exp - 1)},
        )

    for h in range(PIECES):
        pl.when(z + 1 < n_exp)(lambda h=h: tok_copy(1, z, h, tokens).start())
        pl.when(z > 0)(lambda h=h: tok_copy(-1, z, h, tokens).start())

    def comb_copy(k):
        return remote(
            comb.at[z], comb.at[z], comb_ss.at[k], comb_rs.at[z], {"expert": lax.rem(z + k, n_exp)}
        )

    for k in range(1, n_exp):
        comb_copy(k).start()

    for i in range(4):
        loads[i].wait()

    def w_part(side, k):
        return pl.ds(side * half_rows + k * w_rows, w_rows)

    def wx_copy(k):
        part = w_part(y, k)
        ref = w_all.at[own, part]
        return remote(ref, ref, wx_ss.at[k], wx_rs.at[k], {"query": 1 - x})

    def wy_copy(k):
        ref = w_all.at[other, w_part(y, k)]
        return remote(ref, ref, wy_ss.at[k], wy_rs.at[k], {"group": 1 - y})

    def wd_copy(from_y, k):
        ref = w_all.at[other, w_part(1 - y if from_y else y, k)]
        return remote(ref, ref, wd_ss.at[from_y, k], wd_rs.at[from_y, k], {"dp": 1 - c})

    own_copy = remote(w_all.at[own], w_all.at[own], own_ss, own_rs, {"dp": 1 - c})

    for k in range(W_PIECES):
        wx_copy(k).start()
    own_copy.start()

    loads[5].wait()
    loads[6].wait()
    folded = jnp.dot(down_v[...], proj_v[...], preferred_element_type=jnp.float32)
    high = folded.astype(jnp.bfloat16)
    low = (folded - high.astype(jnp.float32)).astype(jnp.bfloat16)
    out_width = proj.shape[1]
    pad_rows = v_all.shape[1] - units
    v_all[own, :units, :out_width] = high
    v_all[own, :units, out_width:] = low
    v_all[own, units:, :] = jnp.zeros((pad_rows, 2 * out_width), jnp.bfloat16)

    loads[4].wait()
    base[...] = jnp.dot(tok[z], proj_v[...], preferred_element_type=jnp.float32)

    v_copies = [
        remote(v_all.at[at], v_all.at[at], v_ss.at[i], v_rs.at[i], who)
        for i, (at, who) in enumerate([(own, {"dp": 1 - c}), (own, {"query": 1 - x}), (other, {"dp": 1 - c})])
    ]
    v_copies[0].start()
    v_copies[1].start()
    q_copy = remote(queries, q_all.at[x], q_ss, q_rs, {"query": 1 - x})
    q_copy.start()

    def product(owner, j, first, count):
        return lax.dot_general(
            tok[owner, :, first : first + count],
            w_all[j, :, first : first + count],
            (((1,), (1,)), ((), ())),
            preferred_element_type=jnp.float32,
        )

    def after(act, j):
        g, u = act[:, :full], act[:, full : 2 * full]
        t = act[:, 2 * full :]
        main = g / (1.0 + jnp.exp(-g)) * u
        last = t / (1.0 + jnp.exp(-t)) * pltpu.roll(t, LANES // 2, 1)
        hidden = jnp.concatenate([main, last], axis=1).astype(jnp.bfloat16)
        both = jnp.dot(hidden, v_all[j], preferred_element_type=jnp.float32)
        return both[:, :out_width] + both[:, out_width:]

    def scale_of(owner, expert):
        pick = jnp.sum(
            jnp.where(row_id == z * 2 + expert, comb[owner], 0.0), axis=0, keepdims=True
        )
        return jnp.broadcast_to(pick, (out_width, rows)).T

    def expert_rows(owner, expert):
        def one(c_at, total):
            j = 2 * expert + c_at
            return total + after(product(owner, j, 0, width), j)

        total = lax.fori_loop(0, 2, one, jnp.zeros((rows, out_width), jnp.float32))
        return total * scale_of(owner, expert)

    own_copy.wait_recv()
    v_copies[0].wait_recv()
    acc[z] = expert_rows(z, x)

    def take(d, h):
        for side in (-1, 1):
            owner = jnp.clip(z + side * d, 0, n_exp - 1)
            inside = (z - d >= 0) if side < 0 else (z + d < n_exp)

            def arrive(side=side, owner=owner):
                tok_copy(1, owner, h).wait_recv()

                if d < n_exp - 1:
                    onward = (z + 1 < n_exp) if side < 0 else (z > 0)
                    pl.when(onward)(lambda: tok_copy(-side, owner, h).start())

            pl.when(inside)(arrive)

    def comb_wait(k):
        src = lax.rem(z + n_exp - k, n_exp)
        remote(
            comb.at[src], comb.at[src], comb_ss.at[k], comb_rs.at[src], {"expert": src}
        ).wait_recv()

    for k in range(1, n_exp):
        comb_wait(k)

    x_taken = 0

    def take_x(k):
        part = w_part(y, k)
        remote(
            w_all.at[other, part], w_all.at[other, part], wx_ss.at[k], wx_rs.at[k], {"query": 1 - x}
        ).wait_recv()
        wy_copy(k).start()
        wd_copy(0, k).start()

    for d in range(1, n_exp - 1):
        for h in range(PIECES):
            take(d, h)
            if (h >= 1 if d == 1 else h == 1) and x_taken < W_PIECES:
                take_x(x_taken)
                x_taken += 1

        def near(owner, _, d=d):
            @pl.when(jnp.abs(owner - z) == d)
            def _():
                acc[owner] = expert_rows(owner, x)

            return 0

        lax.fori_loop(0, n_exp, near, 0)
    while x_taken < W_PIECES:
        take_x(x_taken)
        x_taken += 1

    v_copies[1].wait_recv()
    v_copies[2].start()
    for k in range(W_PIECES):
        part = w_part(1 - y, k)
        ref = w_all.at[other, part]
        remote(ref, ref, wy_ss.at[k], wy_rs.at[k], {"group": 1 - y}).wait_recv()
        wd_copy(1, k).start()
    peer = 2 * (1 - x) + 1 - c
    for from_y in range(2):
        for k in range(W_PIECES):
            ref = w_all.at[peer, w_part(1 - y if from_y else y, k)]
            remote(ref, ref, wd_ss.at[from_y, k], wd_rs.at[from_y, k], {"dp": 1 - c}).wait_recv()
    v_copies[2].wait_recv()

    def far(owner, _):
        @pl.when(jnp.abs(owner - z) < n_exp - 1)
        def _():
            acc[owner] += expert_rows(owner, 1 - x)

        return 0

    lax.fori_loop(0, n_exp, far, 0)

    def ret_copy(owner):
        return remote(
            acc.at[owner], ret.at[z], ret_ss.at[owner], ret_rs.at[z], {"expert": owner}
        )

    def ret_wait(src):
        remote(
            acc.at[src], ret.at[src], ret_ss.at[src], ret_rs.at[src], {"expert": src}
        ).wait_recv()

    for owner in range(n_exp):
        @pl.when(jnp.logical_and(jnp.abs(owner - z) < n_exp - 1, owner != z))
        def _(owner=owner):
            ret_copy(owner).start()

    n_pass, n_lab = out.shape
    n_blocks, q_rows = q_all.shape[0], q_all.shape[1]
    q_len = q_rows * n_blocks // n_lab
    label_at = lax.broadcasted_iota(jnp.int32, (q_rows, LANES), 0) // q_len
    column = lax.broadcasted_iota(jnp.int32, (q_rows, LANES), 1)
    for b in range(n_blocks):
        members[b] = jnp.where(column == label_at + b * (n_lab // n_blocks), 1.0, 0.0).astype(
            jnp.bfloat16
        )
    base[...] += acc[z]

    @pl.when(jnp.logical_or(z == 0, z == n_exp - 1))
    def _():
        owner = n_exp - 1 - z
        scales = [scale_of(owner, e) for e in range(2)]
        for h in range(PIECES):
            tok_copy(1, owner, h).wait_recv()
            if h < PIECES - 1:

                def more(j, _, h=h):
                    term = product(owner, j, h * piece, piece)
                    part_act[j] = term if h == 0 else part_act[j] + term
                    return 0

                lax.fori_loop(0, 4, more, 0)
        total = None
        for e in range(2):
            term = None
            for c_at in range(2):
                j = 2 * e + c_at
                act = part_act[j] + product(owner, j, width - piece, piece)
                term = after(act, j) if term is None else term + after(act, j)
            total = term * scales[e] if total is None else total + term * scales[e]
        acc[owner] = total
        ret_copy(owner).start()

    loads[7].wait()
    q_in = remote(queries, q_all.at[1 - x], q_ss, q_rs, {"query": 1 - x})
    q_in.wait_recv()

    for dist in range(1, n_exp):
        for side in (-1, 1):
            src = z + side * dist
            inside = (src >= 0) if side < 0 else (src < n_exp)

            @pl.when(inside)
            def _(src=jnp.clip(src, 0, n_exp - 1)):
                ret_wait(src)
                base[...] += ret[src]

    projected = base[...]
    norm = jnp.sqrt(jnp.sum(projected * projected, axis=-1, keepdims=True) + 1e-06)
    scaled = projected / norm
    token_at = lax.broadcasted_iota(jnp.int32, (PLEN, out_width), 0)
    live = []
    for p in range(n_pass):
        block = scaled[p * PLEN : (p + 1) * PLEN]
        live.append(jnp.where(token_at < plens[p], block, block[0:1]))
    embedding = jnp.concatenate(live, axis=0).astype(jnp.bfloat16)
    total = jnp.zeros((3 * 8, LANES), jnp.float32)
    for b in range(n_blocks):
        raw = lax.dot_general(
            embedding, q_all[b], (((1,), (1,)), ((), ())), preferred_element_type=jnp.float32
        )
        best = [
            jnp.max(raw[p * PLEN : (p + 1) * PLEN], axis=0, keepdims=True) for p in range(n_pass)
        ]
        best = jnp.concatenate(best + [jnp.zeros((8 - n_pass, q_rows), jnp.float32)], axis=0)
        first = best.astype(jnp.bfloat16).astype(jnp.float32)
        second = (best - first).astype(jnp.bfloat16).astype(jnp.float32)
        third = best - first - second
        parts = jnp.concatenate([first, second, third], axis=0).astype(jnp.bfloat16)
        total += jnp.dot(parts, members[b], preferred_element_type=jnp.float32)
    summed = total[0:8] + total[8:16] + total[16:24]
    out[...] = summed[:n_pass, :n_lab]

    for h in range(PIECES):
        for owner in range(n_exp):
            @pl.when(jnp.logical_and(z + 1 < n_exp, owner <= z))
            def _(owner=owner, h=h):
                tok_copy(1, owner, h).wait_send()

            @pl.when(jnp.logical_and(z > 0, owner >= z))
            def _(owner=owner, h=h):
                tok_copy(-1, owner, h).wait_send()

    for owner in range(n_exp):
        @pl.when(owner != z)
        def _(owner=owner):
            ret_copy(owner).wait_send()

    for k in range(1, n_exp):
        comb_copy(k).wait_send()
    for k in range(W_PIECES):
        wx_copy(k).wait_send()
        wy_copy(k).wait_send()
        wd_copy(0, k).wait_send()
        wd_copy(1, k).wait_send()
    own_copy.wait_send()
    for copy in v_copies:
        copy.wait_send()
    q_copy.wait_send()


def dense_on_device(
    n_exp,
    tokens,
    route_ids,
    gate_values,
    passage_lengths,
    gate_weight,
    up_weight,
    down_weight,
    proj_weight,
    queries,
):
    rows, width = tokens.shape
    units = gate_weight.shape[2]
    out_width = proj_weight.shape[1]
    queries2 = queries.reshape(-1, queries.shape[-1])
    n_experts = n_exp * 2
    v_rows = (units // LANES + 1) * LANES
    any_spec = pl.BlockSpec(memory_space=pl.ANY)
    vmem_spec = pl.BlockSpec(memory_space=pltpu.VMEM)
    dma = pltpu.SemaphoreType.DMA
    bf16, f32 = jnp.bfloat16, jnp.float32
    return pl.pallas_call(
        functools.partial(dense_kernel, n_exp),
        out_shape=jax.ShapeDtypeStruct((passage_lengths.shape[0], queries.shape[0] * 2), f32),
        in_specs=[any_spec] * 6 + [vmem_spec] * 2 + [pl.BlockSpec(memory_space=pltpu.SMEM)],
        out_specs=vmem_spec,
        scratch_shapes=[
            pltpu.VMEM((n_exp, rows, width), bf16),
            pltpu.VMEM((units, width), bf16),
            pltpu.VMEM((width, out_width), bf16),
            pltpu.VMEM((4, 2 * units, width), bf16),
            pltpu.VMEM((4, v_rows, 2 * out_width), bf16),
            pltpu.VMEM((2,) + queries2.shape, bf16),
            pltpu.VMEM((n_exp, n_experts, rows), f32),
            pltpu.VMEM((n_exp, rows, out_width), f32),
            pltpu.VMEM((n_exp, rows, out_width), f32),
            pltpu.VMEM((rows, out_width), f32),
            pltpu.VMEM((4, rows, 2 * units), f32),
            pltpu.VMEM((2, queries2.shape[0], LANES), bf16),
            dma((8,)),
            dma((2, n_exp, PIECES)),
            dma((n_exp, PIECES)),
            dma((n_exp,)),
            dma((n_exp,)),
            dma,
            dma,
            dma((W_PIECES,)),
            dma((W_PIECES,)),
            dma((W_PIECES,)),
            dma((W_PIECES,)),
            dma((2, W_PIECES)),
            dma((2, W_PIECES)),
            dma((3,)),
            dma((3,)),
            dma,
            dma,
            dma((n_exp,)),
            dma((n_exp,)),
        ],
        compiler_params=pltpu.CompilerParams(collective_id=0, has_side_effects=True),
    )(
        tokens,
        gate_weight[0].T,
        up_weight[0].T,
        down_weight[0].T,
        proj_weight,
        queries2,
        route_ids.T,
        gate_values.T,
        passage_lengths,
    )


def dense_fits(mesh_shape, rows, units, top):
    experts = mesh_shape["expert"] * mesh_shape["query"]
    pairs = all(mesh_shape[a] == 2 for a in ("group", "query", "dp"))
    capacity = max(2, 2 * rows * top // experts)
    return pairs and mesh_shape["expert"] > 2 and capacity >= rows and units % LANES == LANES // 2


def passage_scores(embedding, live_mask, block_queries):
    query_rows = block_queries.reshape(-1, block_queries.shape[-1])
    raw_scores = jnp.dot(embedding, query_rows.T, preferred_element_type=jnp.float32)
    raw_scores = jnp.where(live_mask[:, None], raw_scores, -jnp.inf)
    best_match = jnp.max(raw_scores.reshape(-1, PLEN, raw_scores.shape[-1]), axis=1)
    return jnp.sum(best_match.reshape(best_match.shape[0], -1, block_queries.shape[1]), axis=-1)


def on_device(
    tokens,
    route_ids,
    gate_values,
    passage_lengths,
    gate_weight,
    up_weight,
    down_weight,
    proj_weight,
    queries,
):
    tok_rows, model_width = tokens.shape
    top_count = route_ids.shape[1]
    experts = lax.axis_size("expert") * lax.axis_size("query")
    capacity = max(2, 2 * tok_rows * top_count // experts)
    assignments = tok_rows * top_count
    flat_routes = route_ids.reshape(-1)
    one_hot = (flat_routes[:, None] == jnp.arange(experts, dtype=jnp.int32)[None, :]).astype(
        jnp.int32
    )
    earlier = jnp.cumsum(one_hot, axis=0) - one_hot
    slot_index = jnp.sum(earlier * one_hot, axis=1)
    slot_target = flat_routes * capacity + slot_index
    slot_owner = (
        jnp.full((experts * capacity,), assignments, jnp.int32)
        .at[slot_target]
        .set(jnp.arange(assignments, dtype=jnp.int32))
    )
    padded = jnp.concatenate([tokens, jnp.zeros((1, model_width), tokens.dtype)], axis=0)
    source_row = jnp.where(slot_owner < assignments, slot_owner // top_count, tok_rows)
    outgoing = padded[source_row].reshape(experts, capacity, model_width)
    arrived = lax.all_to_all(outgoing, ("expert", "query"), split_axis=0, concat_axis=0, tiled=True)
    expert_rows = arrived.reshape(experts * capacity, model_width)
    gate_act = jnp.dot(
        expert_rows,
        lax.all_gather(gate_weight[0], "dp", axis=1, tiled=True),
        preferred_element_type=jnp.float32,
    )
    up_act = jnp.dot(
        expert_rows,
        lax.all_gather(up_weight[0], "dp", axis=1, tiled=True),
        preferred_element_type=jnp.float32,
    )
    hidden = (jax.nn.silu(gate_act) * up_act).astype(jnp.bfloat16)
    accumulated = lax.dot_general(
        hidden,
        lax.all_gather(down_weight[0], "dp", axis=1, tiled=True),
        (((1,), (1,)), ((), ())),
        preferred_element_type=jnp.float32,
    )
    results = accumulated.astype(jnp.bfloat16)
    weights = gate_values.reshape(assignments, 1)
    folded = jnp.dot(results, proj_weight, preferred_element_type=jnp.float32)
    returned_rows = lax.all_to_all(
        folded.reshape(experts, capacity, folded.shape[-1]),
        ("expert", "query"),
        split_axis=0,
        concat_axis=0,
        tiled=True,
    )
    picked = returned_rows.reshape(experts * capacity, folded.shape[-1])[slot_target]
    projected = jnp.dot(tokens, proj_weight, preferred_element_type=jnp.float32) + jnp.sum(
        (picked * weights).reshape(tok_rows, top_count, folded.shape[-1]), axis=1
    )
    lengths_norm = jnp.sqrt(jnp.sum(projected * projected, axis=-1, keepdims=True) + 1e-06)
    embedding = (projected / lengths_norm).astype(jnp.bfloat16)
    position = jnp.arange(tok_rows, dtype=jnp.int32) % PLEN
    live_mask = position < jnp.repeat(passage_lengths, PLEN)
    return passage_scores(
        embedding, live_mask, lax.all_gather(queries, "query", axis=0, tiled=True)
    )


def solution(mesh):
    in_specs = (
        P(("group", "expert", "query", "dp"), None),
        P(("group", "expert", "query", "dp"), None),
        P(("group", "expert", "query", "dp"), None),
        P(("group", "expert", "query", "dp")),
        P(("expert", "query"), None, "dp"),
        P(("expert", "query"), None, "dp"),
        P(("expert", "query"), None, "dp"),
        P(),
        P(("group", "query"), None, None),
    )
    out_specs = P(("group", "expert", "query", "dp"), None)
    sizes = dict(mesh.shape)

    def run(tokens, route_ids, *rest):
        units = rest[2].shape[2]
        if dense_fits(sizes, tokens.shape[0], units, route_ids.shape[1]):
            return dense_on_device(sizes["expert"], tokens, route_ids, *rest)
        return on_device(tokens, route_ids, *rest)

    return jax.shard_map(
        run, mesh=mesh, in_specs=in_specs, out_specs=out_specs, check_vma=False
    )
```

```python
import functools

import jax
import jax.numpy as jnp
from jax import lax
from jax.experimental import pallas as pl
from jax.experimental.pallas import tpu as pltpu
from jax.sharding import PartitionSpec as P

PLEN = 64
MESH = pl.DeviceIdType.MESH
LANES = 128
PIECES = 4
W_PIECES = 4


def dense_kernel(
    n_exp,
    tokens,
    gate,
    up,
    down,
    proj,
    queries,
    routes,
    gates,
    plens,
    out,
    tok,
    down_v,
    proj_v,
    w_all,
    v_all,
    q_all,
    comb,
    acc,
    ret,
    base,
    part_act,
    members,
    local_sem,
    tok_ss,
    tok_rs,
    comb_ss,
    comb_rs,
    own_ss,
    own_rs,
    wx_ss,
    wx_rs,
    wy_ss,
    wy_rs,
    wd_ss,
    wd_rs,
    v_ss,
    v_rs,
    q_ss,
    q_rs,
    ret_ss,
    ret_rs,
):
    z, x = lax.axis_index("expert"), lax.axis_index("query")
    y, c = lax.axis_index("group"), lax.axis_index("dp")
    rows, width = tokens.shape
    units = gate.shape[0]
    full = units // LANES * LANES
    piece = width // PIECES
    half_rows = units
    w_rows = half_rows // W_PIECES
    own = 2 * x + c
    other = 2 * (1 - x) + c
    ends = 2 * full + units - full
    top = routes.shape[0]

    w_own = w_all.at[own]
    arranged = [
        (gate.at[:full], w_own.at[:full]),
        (up.at[:full], w_own.at[full : 2 * full]),
        (gate.at[full:], w_own.at[2 * full : ends]),
        (up.at[full:], w_own.at[ends:]),
        (tokens, tok.at[z]),
        (down, down_v),
        (proj, proj_v),
        (queries, q_all.at[x]),
    ]
    loads = [
        pltpu.make_async_copy(src, dst, local_sem.at[i]) for i, (src, dst) in enumerate(arranged)
    ]
    for load in loads:
        load.start()

    barrier = pltpu.get_barrier_semaphore()
    partners = [{"dp": 1 - c}, {"query": 1 - x}, {"group": 1 - y}]
    for who in partners:
        pl.semaphore_signal(barrier, inc=1, device_id=who, device_id_type=MESH)
    beside = [(z + 1 < n_exp, {"expert": z + 1}), (z > 0, {"expert": z - 1})]
    for there, who in beside:

        @pl.when(there)
        def _(who=who):
            pl.semaphore_signal(barrier, inc=1, device_id=who, device_id_type=MESH)

    row_id = lax.broadcasted_iota(jnp.int32, comb.shape[1:], 0)
    spread = jnp.zeros(comb.shape[1:], jnp.float32)
    for k in range(top):
        spread += jnp.where(routes[k : k + 1, :] == row_id, gates[k : k + 1, :], 0.0)
    comb[z] = spread
    at_end = jnp.logical_or(z == 0, z == n_exp - 1)
    pl.semaphore_wait(barrier, jnp.where(at_end, len(partners) + 1, len(partners) + 2))

    def remote(src, dst, ss, rs, who):
        return pltpu.make_async_remote_copy(
            src_ref=src, dst_ref=dst, send_sem=ss, recv_sem=rs, device_id=who, device_id_type=MESH
        )

    def tok_copy(step, owner, h, src=None):
        part = pl.ds(h * piece, piece)
        dst = tok.at[owner, :, part]
        return remote(
            dst if src is None else src.at[:, part],
            dst,
            tok_ss.at[(step + 1) // 2, owner, h],
            tok_rs.at[owner, h],
            {"expert": jnp.clip(z + step, 0, n_exp - 1)},
        )

    for h in range(PIECES):
        pl.when(z + 1 < n_exp)(lambda h=h: tok_copy(1, z, h, tokens).start())
        pl.when(z > 0)(lambda h=h: tok_copy(-1, z, h, tokens).start())

    def comb_copy(step, owner):
        ref = comb.at[owner]
        return remote(
            ref,
            ref,
            comb_ss.at[(step + 1) // 2, owner],
            comb_rs.at[owner],
            {"expert": jnp.clip(z + step, 0, n_exp - 1)},
        )

    pl.when(z + 1 < n_exp)(lambda: comb_copy(1, z).start())
    pl.when(z > 0)(lambda: comb_copy(-1, z).start())

    for i in range(4):
        loads[i].wait()

    def w_part(side, k):
        return pl.ds(side * half_rows + k * w_rows, w_rows)

    def wx_copy(k):
        part = w_part(y, k)
        ref = w_all.at[own, part]
        return remote(ref, ref, wx_ss.at[k], wx_rs.at[k], {"query": 1 - x})

    def wy_copy(k):
        ref = w_all.at[other, w_part(y, k)]
        return remote(ref, ref, wy_ss.at[k], wy_rs.at[k], {"group": 1 - y})

    def wd_copy(from_y, k):
        ref = w_all.at[other, w_part(1 - y if from_y else y, k)]
        return remote(ref, ref, wd_ss.at[from_y, k], wd_rs.at[from_y, k], {"dp": 1 - c})

    own_copy = remote(w_all.at[own], w_all.at[own], own_ss, own_rs, {"dp": 1 - c})

    for k in range(W_PIECES):
        wx_copy(k).start()
    own_copy.start()

    loads[5].wait()
    loads[6].wait()
    folded = jnp.dot(down_v[...], proj_v[...], preferred_element_type=jnp.float32)
    high = folded.astype(jnp.bfloat16)
    low = (folded - high.astype(jnp.float32)).astype(jnp.bfloat16)
    out_width = proj.shape[1]
    pad_rows = v_all.shape[1] - units
    v_all[own, :units, :out_width] = high
    v_all[own, :units, out_width:] = low
    v_all[own, units:, :] = jnp.zeros((pad_rows, 2 * out_width), jnp.bfloat16)

    loads[4].wait()
    base[...] = jnp.dot(tok[z], proj_v[...], preferred_element_type=jnp.float32)

    v_copies = [
        remote(v_all.at[at], v_all.at[at], v_ss.at[i], v_rs.at[i], who)
        for i, (at, who) in enumerate([(own, {"dp": 1 - c}), (own, {"query": 1 - x}), (other, {"dp": 1 - c})])
    ]
    v_copies[0].start()
    v_copies[1].start()
    q_copy = remote(queries, q_all.at[x], q_ss, q_rs, {"query": 1 - x})
    q_copy.start()

    def product(owner, j, first, count):
        return lax.dot_general(
            tok[owner, :, first : first + count],
            w_all[j, :, first : first + count],
            (((1,), (1,)), ((), ())),
            preferred_element_type=jnp.float32,
        )

    def after(act, j):
        g, u = act[:, :full], act[:, full : 2 * full]
        t = act[:, 2 * full :]
        main = g / (1.0 + jnp.exp(-g)) * u
        last = t / (1.0 + jnp.exp(-t)) * pltpu.roll(t, LANES // 2, 1)
        hidden = jnp.concatenate([main, last], axis=1).astype(jnp.bfloat16)
        both = jnp.dot(hidden, v_all[j], preferred_element_type=jnp.float32)
        return both[:, :out_width] + both[:, out_width:]

    def scale_of(owner, expert):
        pick = jnp.sum(
            jnp.where(row_id == z * 2 + expert, comb[owner], 0.0), axis=0, keepdims=True
        )
        return jnp.broadcast_to(pick, (out_width, rows)).T

    def expert_rows(owner, expert):
        def one(c_at, total):
            j = 2 * expert + c_at
            return total + after(product(owner, j, 0, width), j)

        total = lax.fori_loop(0, 2, one, jnp.zeros((rows, out_width), jnp.float32))
        return total * scale_of(owner, expert)

    own_copy.wait_recv()
    v_copies[0].wait_recv()
    acc[z] = expert_rows(z, x)

    def take(d, h):
        for side in (-1, 1):
            owner = jnp.clip(z + side * d, 0, n_exp - 1)
            inside = (z - d >= 0) if side < 0 else (z + d < n_exp)

            def arrive(side=side, owner=owner):
                onward = (z + 1 < n_exp) if side < 0 else (z > 0)
                tok_copy(1, owner, h).wait_recv()
                pl.when(onward)(lambda: tok_copy(-side, owner, h).start())
                if h == 0:
                    comb_copy(1, owner).wait_recv()
                    pl.when(onward)(lambda: comb_copy(-side, owner).start())

            pl.when(inside)(arrive)

    x_taken = 0

    def take_x(k):
        part = w_part(y, k)
        remote(
            w_all.at[other, part], w_all.at[other, part], wx_ss.at[k], wx_rs.at[k], {"query": 1 - x}
        ).wait_recv()
        wy_copy(k).start()
        wd_copy(0, k).start()

    for d in range(1, n_exp - 1):
        for h in range(PIECES):
            take(d, h)
            if (h >= 1 if d == 1 else h == 1) and x_taken < W_PIECES:
                take_x(x_taken)
                x_taken += 1

        def near(owner, _, d=d):
            @pl.when(jnp.abs(owner - z) == d)
            def _():
                acc[owner] = expert_rows(owner, x)

            return 0

        lax.fori_loop(0, n_exp, near, 0)
    while x_taken < W_PIECES:
        take_x(x_taken)
        x_taken += 1

    v_copies[1].wait_recv()
    v_copies[2].start()
    for k in range(W_PIECES):
        part = w_part(1 - y, k)
        ref = w_all.at[other, part]
        remote(ref, ref, wy_ss.at[k], wy_rs.at[k], {"group": 1 - y}).wait_recv()
        wd_copy(1, k).start()
    peer = 2 * (1 - x) + 1 - c
    for from_y in range(2):
        for k in range(W_PIECES):
            ref = w_all.at[peer, w_part(1 - y if from_y else y, k)]
            remote(ref, ref, wd_ss.at[from_y, k], wd_rs.at[from_y, k], {"dp": 1 - c}).wait_recv()
    v_copies[2].wait_recv()

    many = n_exp - 1
    start = jnp.where(z == n_exp - 1, 1, 0)
    window = pl.ds(start, many)
    rows_in = tok[window].reshape(many * rows, width)

    def far(c_at, total):
        j = 2 * (1 - x) + c_at
        act = lax.dot_general(
            rows_in, w_all[j], (((1,), (1,)), ((), ())), preferred_element_type=jnp.float32
        )
        return total + after(act, j)

    total = lax.fori_loop(0, 2, far, jnp.zeros((many * rows, out_width), jnp.float32))
    scales = jnp.concatenate([scale_of(start + i, 1 - x) for i in range(many)], axis=0)
    acc[window] += (total * scales).reshape(many, rows, out_width)

    @pl.when(jnp.logical_and(z > 0, z < n_exp - 1))
    def _():
        acc[n_exp - 1] += expert_rows(n_exp - 1, 1 - x)

    def ret_copy(owner):
        return remote(
            acc.at[owner], ret.at[z], ret_ss.at[owner], ret_rs.at[z], {"expert": owner}
        )

    def ret_wait(src):
        remote(
            acc.at[src], ret.at[src], ret_ss.at[src], ret_rs.at[src], {"expert": src}
        ).wait_recv()

    for owner in range(n_exp):
        @pl.when(jnp.logical_and(jnp.abs(owner - z) < n_exp - 1, owner != z))
        def _(owner=owner):
            ret_copy(owner).start()

    n_pass, n_lab = out.shape
    n_blocks, q_rows = q_all.shape[0], q_all.shape[1]
    q_len = q_rows * n_blocks // n_lab
    label_at = lax.broadcasted_iota(jnp.int32, (q_rows, LANES), 0) // q_len
    column = lax.broadcasted_iota(jnp.int32, (q_rows, LANES), 1)
    for b in range(n_blocks):
        members[b] = jnp.where(column == label_at + b * (n_lab // n_blocks), 1.0, 0.0).astype(
            jnp.bfloat16
        )
    base[...] += acc[z]

    @pl.when(jnp.logical_or(z == 0, z == n_exp - 1))
    def _():
        owner = n_exp - 1 - z
        comb_copy(1, owner).wait_recv()
        scales = [scale_of(owner, e) for e in range(2)]
        for h in range(PIECES):
            tok_copy(1, owner, h).wait_recv()
            if h < PIECES - 1:

                def more(j, _, h=h):
                    term = product(owner, j, h * piece, piece)
                    part_act[j] = term if h == 0 else part_act[j] + term
                    return 0

                lax.fori_loop(0, 4, more, 0)
        total = None
        for e in range(2):
            term = None
            for c_at in range(2):
                j = 2 * e + c_at
                act = part_act[j] + product(owner, j, width - piece, piece)
                term = after(act, j) if term is None else term + after(act, j)
            total = term * scales[e] if total is None else total + term * scales[e]
        acc[owner] = total
        ret_copy(owner).start()

    loads[7].wait()
    q_in = remote(queries, q_all.at[1 - x], q_ss, q_rs, {"query": 1 - x})
    q_in.wait_recv()

    for dist in range(1, n_exp):
        for side in (-1, 1):
            src = z + side * dist
            inside = (src >= 0) if side < 0 else (src < n_exp)

            @pl.when(inside)
            def _(src=jnp.clip(src, 0, n_exp - 1)):
                ret_wait(src)
                base[...] += ret[src]

    projected = base[...]
    norm = jnp.sqrt(jnp.sum(projected * projected, axis=-1, keepdims=True) + 1e-06)
    scaled = projected / norm
    token_at = lax.broadcasted_iota(jnp.int32, (PLEN, out_width), 0)
    live = []
    for p in range(n_pass):
        block = scaled[p * PLEN : (p + 1) * PLEN]
        live.append(jnp.where(token_at < plens[p], block, block[0:1]))
    embedding = jnp.concatenate(live, axis=0).astype(jnp.bfloat16)
    total = jnp.zeros((3 * 8, LANES), jnp.float32)
    for b in range(n_blocks):
        raw = lax.dot_general(
            embedding, q_all[b], (((1,), (1,)), ((), ())), preferred_element_type=jnp.float32
        )
        best = [
            jnp.max(raw[p * PLEN : (p + 1) * PLEN], axis=0, keepdims=True) for p in range(n_pass)
        ]
        best = jnp.concatenate(best + [jnp.zeros((8 - n_pass, q_rows), jnp.float32)], axis=0)
        first = best.astype(jnp.bfloat16).astype(jnp.float32)
        second = (best - first).astype(jnp.bfloat16).astype(jnp.float32)
        third = best - first - second
        parts = jnp.concatenate([first, second, third], axis=0).astype(jnp.bfloat16)
        total += jnp.dot(parts, members[b], preferred_element_type=jnp.float32)
    summed = total[0:8] + total[8:16] + total[16:24]
    out[...] = summed[:n_pass, :n_lab]

    for owner in range(n_exp):
        pl.when(jnp.logical_and(z + 1 < n_exp, owner <= z))(
            lambda owner=owner: comb_copy(1, owner).wait_send()
        )
        pl.when(jnp.logical_and(z > 0, owner >= z))(
            lambda owner=owner: comb_copy(-1, owner).wait_send()
        )
    for h in range(PIECES):
        for owner in range(n_exp):
            @pl.when(jnp.logical_and(z + 1 < n_exp, owner <= z))
            def _(owner=owner, h=h):
                tok_copy(1, owner, h).wait_send()

            @pl.when(jnp.logical_and(z > 0, owner >= z))
            def _(owner=owner, h=h):
                tok_copy(-1, owner, h).wait_send()

    for owner in range(n_exp):
        @pl.when(owner != z)
        def _(owner=owner):
            ret_copy(owner).wait_send()

    for k in range(W_PIECES):
        wx_copy(k).wait_send()
        wy_copy(k).wait_send()
        wd_copy(0, k).wait_send()
        wd_copy(1, k).wait_send()
    own_copy.wait_send()
    for copy in v_copies:
        copy.wait_send()
    q_copy.wait_send()


def dense_on_device(
    n_exp,
    tokens,
    route_ids,
    gate_values,
    passage_lengths,
    gate_weight,
    up_weight,
    down_weight,
    proj_weight,
    queries,
):
    rows, width = tokens.shape
    units = gate_weight.shape[2]
    out_width = proj_weight.shape[1]
    queries2 = queries.reshape(-1, queries.shape[-1])
    n_experts = n_exp * 2
    v_rows = (units // LANES + 1) * LANES
    any_spec = pl.BlockSpec(memory_space=pl.ANY)
    vmem_spec = pl.BlockSpec(memory_space=pltpu.VMEM)
    dma = pltpu.SemaphoreType.DMA
    bf16, f32 = jnp.bfloat16, jnp.float32
    return pl.pallas_call(
        functools.partial(dense_kernel, n_exp),
        out_shape=jax.ShapeDtypeStruct((passage_lengths.shape[0], queries.shape[0] * 2), f32),
        in_specs=[any_spec] * 6 + [vmem_spec] * 2 + [pl.BlockSpec(memory_space=pltpu.SMEM)],
        out_specs=vmem_spec,
        scratch_shapes=[
            pltpu.VMEM((n_exp, rows, width), bf16),
            pltpu.VMEM((units, width), bf16),
            pltpu.VMEM((width, out_width), bf16),
            pltpu.VMEM((4, 2 * units, width), bf16),
            pltpu.VMEM((4, v_rows, 2 * out_width), bf16),
            pltpu.VMEM((2,) + queries2.shape, bf16),
            pltpu.VMEM((n_exp, n_experts, rows), f32),
            pltpu.VMEM((n_exp, rows, out_width), f32),
            pltpu.VMEM((n_exp, rows, out_width), f32),
            pltpu.VMEM((rows, out_width), f32),
            pltpu.VMEM((4, rows, 2 * units), f32),
            pltpu.VMEM((2, queries2.shape[0], LANES), bf16),
            dma((8,)),
            dma((2, n_exp, PIECES)),
            dma((n_exp, PIECES)),
            dma((2, n_exp)),
            dma((n_exp,)),
            dma,
            dma,
            dma((W_PIECES,)),
            dma((W_PIECES,)),
            dma((W_PIECES,)),
            dma((W_PIECES,)),
            dma((2, W_PIECES)),
            dma((2, W_PIECES)),
            dma((3,)),
            dma((3,)),
            dma,
            dma,
            dma((n_exp,)),
            dma((n_exp,)),
        ],
        compiler_params=pltpu.CompilerParams(collective_id=0, has_side_effects=True),
    )(
        tokens,
        gate_weight[0].T,
        up_weight[0].T,
        down_weight[0].T,
        proj_weight,
        queries2,
        route_ids.T,
        gate_values.T,
        passage_lengths,
    )


def dense_fits(mesh_shape, rows, units, top):
    experts = mesh_shape["expert"] * mesh_shape["query"]
    pairs = all(mesh_shape[a] == 2 for a in ("group", "query", "dp"))
    capacity = max(2, 2 * rows * top // experts)
    return pairs and mesh_shape["expert"] > 2 and capacity >= rows and units % LANES == LANES // 2


def passage_scores(embedding, live_mask, block_queries):
    query_rows = block_queries.reshape(-1, block_queries.shape[-1])
    raw_scores = jnp.dot(embedding, query_rows.T, preferred_element_type=jnp.float32)
    raw_scores = jnp.where(live_mask[:, None], raw_scores, -jnp.inf)
    best_match = jnp.max(raw_scores.reshape(-1, PLEN, raw_scores.shape[-1]), axis=1)
    return jnp.sum(best_match.reshape(best_match.shape[0], -1, block_queries.shape[1]), axis=-1)


def on_device(
    tokens,
    route_ids,
    gate_values,
    passage_lengths,
    gate_weight,
    up_weight,
    down_weight,
    proj_weight,
    queries,
):
    tok_rows, model_width = tokens.shape
    top_count = route_ids.shape[1]
    experts = lax.axis_size("expert") * lax.axis_size("query")
    capacity = max(2, 2 * tok_rows * top_count // experts)
    assignments = tok_rows * top_count
    flat_routes = route_ids.reshape(-1)
    one_hot = (flat_routes[:, None] == jnp.arange(experts, dtype=jnp.int32)[None, :]).astype(
        jnp.int32
    )
    earlier = jnp.cumsum(one_hot, axis=0) - one_hot
    slot_index = jnp.sum(earlier * one_hot, axis=1)
    slot_target = flat_routes * capacity + slot_index
    slot_owner = (
        jnp.full((experts * capacity,), assignments, jnp.int32)
        .at[slot_target]
        .set(jnp.arange(assignments, dtype=jnp.int32))
    )
    padded = jnp.concatenate([tokens, jnp.zeros((1, model_width), tokens.dtype)], axis=0)
    source_row = jnp.where(slot_owner < assignments, slot_owner // top_count, tok_rows)
    outgoing = padded[source_row].reshape(experts, capacity, model_width)
    arrived = lax.all_to_all(outgoing, ("expert", "query"), split_axis=0, concat_axis=0, tiled=True)
    expert_rows = arrived.reshape(experts * capacity, model_width)
    gate_act = jnp.dot(
        expert_rows,
        lax.all_gather(gate_weight[0], "dp", axis=1, tiled=True),
        preferred_element_type=jnp.float32,
    )
    up_act = jnp.dot(
        expert_rows,
        lax.all_gather(up_weight[0], "dp", axis=1, tiled=True),
        preferred_element_type=jnp.float32,
    )
    hidden = (jax.nn.silu(gate_act) * up_act).astype(jnp.bfloat16)
    accumulated = lax.dot_general(
        hidden,
        lax.all_gather(down_weight[0], "dp", axis=1, tiled=True),
        (((1,), (1,)), ((), ())),
        preferred_element_type=jnp.float32,
    )
    results = accumulated.astype(jnp.bfloat16)
    weights = gate_values.reshape(assignments, 1)
    folded = jnp.dot(results, proj_weight, preferred_element_type=jnp.float32)
    returned_rows = lax.all_to_all(
        folded.reshape(experts, capacity, folded.shape[-1]),
        ("expert", "query"),
        split_axis=0,
        concat_axis=0,
        tiled=True,
    )
    picked = returned_rows.reshape(experts * capacity, folded.shape[-1])[slot_target]
    projected = jnp.dot(tokens, proj_weight, preferred_element_type=jnp.float32) + jnp.sum(
        (picked * weights).reshape(tok_rows, top_count, folded.shape[-1]), axis=1
    )
    lengths_norm = jnp.sqrt(jnp.sum(projected * projected, axis=-1, keepdims=True) + 1e-06)
    embedding = (projected / lengths_norm).astype(jnp.bfloat16)
    position = jnp.arange(tok_rows, dtype=jnp.int32) % PLEN
    live_mask = position < jnp.repeat(passage_lengths, PLEN)
    return passage_scores(
        embedding, live_mask, lax.all_gather(queries, "query", axis=0, tiled=True)
    )


def solution(mesh):
    in_specs = (
        P(("group", "expert", "query", "dp"), None),
        P(("group", "expert", "query", "dp"), None),
        P(("group", "expert", "query", "dp"), None),
        P(("group", "expert", "query", "dp")),
        P(("expert", "query"), None, "dp"),
        P(("expert", "query"), None, "dp"),
        P(("expert", "query"), None, "dp"),
        P(),
        P(("group", "query"), None, None),
    )
    out_specs = P(("group", "expert", "query", "dp"), None)
    sizes = dict(mesh.shape)

    def run(tokens, route_ids, *rest):
        units = rest[2].shape[2]
        if dense_fits(sizes, tokens.shape[0], units, route_ids.shape[1]):
            return dense_on_device(sizes["expert"], tokens, route_ids, *rest)
        return on_device(tokens, route_ids, *rest)

    return jax.shard_map(
        run, mesh=mesh, in_specs=in_specs, out_specs=out_specs, check_vma=False
    )
```

```python
import functools

import jax
import jax.numpy as jnp
from jax import lax
from jax.experimental import pallas as pl
from jax.experimental.pallas import tpu as pltpu
from jax.sharding import PartitionSpec as P

PLEN = 64
MESH = pl.DeviceIdType.MESH
LANES = 128
PIECES = 4
W_PIECES = 4


def dense_kernel(
    n_exp,
    tokens,
    gate,
    up,
    down,
    proj,
    queries,
    routes,
    gates,
    plens,
    out,
    tok,
    down_v,
    proj_v,
    w_all,
    v_all,
    q_all,
    comb,
    acc,
    ret,
    base,
    part_act,
    members,
    local_sem,
    tok_ss,
    tok_rs,
    comb_ss,
    comb_rs,
    own_ss,
    own_rs,
    wx_ss,
    wx_rs,
    wy_ss,
    wy_rs,
    wd_ss,
    wd_rs,
    v_ss,
    v_rs,
    q_ss,
    q_rs,
    ret_ss,
    ret_rs,
):
    z, x = lax.axis_index("expert"), lax.axis_index("query")
    y, c = lax.axis_index("group"), lax.axis_index("dp")
    rows, width = tokens.shape
    units = gate.shape[0]
    full = units // LANES * LANES
    piece = width // PIECES
    half_rows = units
    w_rows = half_rows // W_PIECES
    own = 2 * x + c
    other = 2 * (1 - x) + c
    ends = 2 * full + units - full
    top = routes.shape[0]

    w_own = w_all.at[own]
    arranged = [
        (gate.at[:full], w_own.at[:full]),
        (up.at[:full], w_own.at[full : 2 * full]),
        (gate.at[full:], w_own.at[2 * full : ends]),
        (up.at[full:], w_own.at[ends:]),
        (tokens, tok.at[z]),
        (down, down_v),
        (proj, proj_v),
        (queries, q_all.at[x]),
    ]
    loads = [
        pltpu.make_async_copy(src, dst, local_sem.at[i]) for i, (src, dst) in enumerate(arranged)
    ]
    for load in loads:
        load.start()

    barrier = pltpu.get_barrier_semaphore()
    partners = [{"dp": 1 - c}, {"query": 1 - x}, {"group": 1 - y}]
    for who in partners:
        pl.semaphore_signal(barrier, inc=1, device_id=who, device_id_type=MESH)
    beside = [(z + 1 < n_exp, {"expert": z + 1}), (z > 0, {"expert": z - 1})]
    for there, who in beside:

        @pl.when(there)
        def _(who=who):
            pl.semaphore_signal(barrier, inc=1, device_id=who, device_id_type=MESH)

    row_id = lax.broadcasted_iota(jnp.int32, comb.shape[1:], 0)
    spread = jnp.zeros(comb.shape[1:], jnp.float32)
    for k in range(top):
        spread += jnp.where(routes[k : k + 1, :] == row_id, gates[k : k + 1, :], 0.0)
    comb[z] = spread
    at_end = jnp.logical_or(z == 0, z == n_exp - 1)
    pl.semaphore_wait(barrier, jnp.where(at_end, len(partners) + 1, len(partners) + 2))

    def remote(src, dst, ss, rs, who):
        return pltpu.make_async_remote_copy(
            src_ref=src, dst_ref=dst, send_sem=ss, recv_sem=rs, device_id=who, device_id_type=MESH
        )

    def tok_copy(step, owner, h, src=None):
        part = pl.ds(h * piece, piece)
        dst = tok.at[owner, :, part]
        return remote(
            dst if src is None else src.at[:, part],
            dst,
            tok_ss.at[(step + 1) // 2, owner, h],
            tok_rs.at[owner, h],
            {"expert": jnp.clip(z + step, 0, n_exp - 1)},
        )

    for h in range(PIECES):
        pl.when(z + 1 < n_exp)(lambda h=h: tok_copy(1, z, h, tokens).start())
        pl.when(z > 0)(lambda h=h: tok_copy(-1, z, h, tokens).start())

    def comb_copy(step, owner):
        ref = comb.at[owner]
        return remote(
            ref,
            ref,
            comb_ss.at[(step + 1) // 2, owner],
            comb_rs.at[owner],
            {"expert": jnp.clip(z + step, 0, n_exp - 1)},
        )

    pl.when(z + 1 < n_exp)(lambda: comb_copy(1, z).start())
    pl.when(z > 0)(lambda: comb_copy(-1, z).start())

    for i in range(4):
        loads[i].wait()

    def w_part(side, k):
        return pl.ds(side * half_rows + k * w_rows, w_rows)

    def wx_copy(k):
        part = w_part(y, k)
        ref = w_all.at[own, part]
        return remote(ref, ref, wx_ss.at[k], wx_rs.at[k], {"query": 1 - x})

    def wy_copy(k):
        ref = w_all.at[other, w_part(y, k)]
        return remote(ref, ref, wy_ss.at[k], wy_rs.at[k], {"group": 1 - y})

    def wd_copy(from_y, k):
        ref = w_all.at[other, w_part(1 - y if from_y else y, k)]
        return remote(ref, ref, wd_ss.at[from_y, k], wd_rs.at[from_y, k], {"dp": 1 - c})

    own_copy = remote(w_all.at[own], w_all.at[own], own_ss, own_rs, {"dp": 1 - c})

    for k in range(W_PIECES):
        wx_copy(k).start()
    own_copy.start()

    loads[5].wait()
    loads[6].wait()
    folded = jnp.dot(down_v[...], proj_v[...], preferred_element_type=jnp.float32)
    high = folded.astype(jnp.bfloat16)
    low = (folded - high.astype(jnp.float32)).astype(jnp.bfloat16)
    out_width = proj.shape[1]
    pad_rows = v_all.shape[1] - units
    v_all[own, :units, :out_width] = high
    v_all[own, :units, out_width:] = low
    v_all[own, units:, :] = jnp.zeros((pad_rows, 2 * out_width), jnp.bfloat16)

    loads[4].wait()
    base[...] = jnp.dot(tok[z], proj_v[...], preferred_element_type=jnp.float32)

    v_copies = [
        remote(v_all.at[at], v_all.at[at], v_ss.at[i], v_rs.at[i], who)
        for i, (at, who) in enumerate([(own, {"dp": 1 - c}), (own, {"query": 1 - x}), (other, {"dp": 1 - c})])
    ]
    v_copies[0].start()
    v_copies[1].start()
    q_copy = remote(queries, q_all.at[x], q_ss, q_rs, {"query": 1 - x})
    q_copy.start()

    def product(owner, j, first, count):
        return lax.dot_general(
            tok[owner, :, first : first + count],
            w_all[j, :, first : first + count],
            (((1,), (1,)), ((), ())),
            preferred_element_type=jnp.float32,
        )

    def after(act, j):
        g, u = act[:, :full], act[:, full : 2 * full]
        t = act[:, 2 * full :]
        main = g / (1.0 + jnp.exp(-g)) * u
        last = t / (1.0 + jnp.exp(-t)) * pltpu.roll(t, LANES // 2, 1)
        hidden = jnp.concatenate([main, last], axis=1).astype(jnp.bfloat16)
        both = jnp.dot(hidden, v_all[j], preferred_element_type=jnp.float32)
        return both[:, :out_width] + both[:, out_width:]

    def scale_of(owner, expert):
        pick = jnp.sum(
            jnp.where(row_id == z * 2 + expert, comb[owner], 0.0), axis=0, keepdims=True
        )
        return jnp.broadcast_to(pick, (out_width, rows)).T

    def expert_rows(owner, expert):
        def one(c_at, total):
            j = 2 * expert + c_at
            return total + after(product(owner, j, 0, width), j)

        total = lax.fori_loop(0, 2, one, jnp.zeros((rows, out_width), jnp.float32))
        return total * scale_of(owner, expert)

    own_copy.wait_recv()
    v_copies[0].wait_recv()
    acc[z] = expert_rows(z, x)

    def take(d, h):
        for side in (-1, 1):
            owner = jnp.clip(z + side * d, 0, n_exp - 1)
            inside = (z - d >= 0) if side < 0 else (z + d < n_exp)

            def arrive(side=side, owner=owner):
                onward = (z + 1 < n_exp) if side < 0 else (z > 0)
                tok_copy(1, owner, h).wait_recv()
                pl.when(onward)(lambda: tok_copy(-side, owner, h).start())
                if h == 0:
                    comb_copy(1, owner).wait_recv()
                    pl.when(onward)(lambda: comb_copy(-side, owner).start())

            pl.when(inside)(arrive)

    x_taken = 0

    def take_x(k):
        part = w_part(y, k)
        remote(
            w_all.at[other, part], w_all.at[other, part], wx_ss.at[k], wx_rs.at[k], {"query": 1 - x}
        ).wait_recv()
        wy_copy(k).start()
        wd_copy(0, k).start()

    for d in range(1, n_exp - 1):
        for h in range(PIECES):
            take(d, h)
            if (h >= 1 if d == 1 else h == 1) and x_taken < W_PIECES:
                take_x(x_taken)
                x_taken += 1

        def near(owner, _, d=d):
            @pl.when(jnp.abs(owner - z) == d)
            def _():
                acc[owner] = expert_rows(owner, x)

            return 0

        lax.fori_loop(0, n_exp, near, 0)
    while x_taken < W_PIECES:
        take_x(x_taken)
        x_taken += 1

    v_copies[1].wait_recv()
    v_copies[2].start()
    for k in range(W_PIECES):
        part = w_part(1 - y, k)
        ref = w_all.at[other, part]
        remote(ref, ref, wy_ss.at[k], wy_rs.at[k], {"group": 1 - y}).wait_recv()
        wd_copy(1, k).start()
    peer = 2 * (1 - x) + 1 - c
    for from_y in range(2):
        for k in range(W_PIECES):
            ref = w_all.at[peer, w_part(1 - y if from_y else y, k)]
            remote(ref, ref, wd_ss.at[from_y, k], wd_rs.at[from_y, k], {"dp": 1 - c}).wait_recv()
    v_copies[2].wait_recv()

    many = n_exp - 1
    start = jnp.where(z == n_exp - 1, 1, 0)
    window = pl.ds(start, many)
    rows_in = tok[window].reshape(many * rows, width)

    def far(c_at, total):
        j = 2 * (1 - x) + c_at
        act = lax.dot_general(
            rows_in, w_all[j], (((1,), (1,)), ((), ())), preferred_element_type=jnp.float32
        )
        return total + after(act, j)

    total = lax.fori_loop(0, 2, far, jnp.zeros((many * rows, out_width), jnp.float32))
    scales = jnp.concatenate([scale_of(start + i, 1 - x) for i in range(many)], axis=0)
    acc[window] += (total * scales).reshape(many, rows, out_width)

    @pl.when(jnp.logical_and(z > 0, z < n_exp - 1))
    def _():
        acc[n_exp - 1] += expert_rows(n_exp - 1, 1 - x)

    def ret_copy(owner):
        return remote(
            acc.at[owner], ret.at[z], ret_ss.at[owner], ret_rs.at[z], {"expert": owner}
        )

    def ret_wait(src):
        remote(
            acc.at[src], ret.at[src], ret_ss.at[src], ret_rs.at[src], {"expert": src}
        ).wait_recv()

    for owner in range(n_exp):
        @pl.when(jnp.logical_and(jnp.abs(owner - z) < n_exp - 1, owner != z))
        def _(owner=owner):
            ret_copy(owner).start()

    n_pass, n_lab = out.shape
    n_blocks, q_rows = q_all.shape[0], q_all.shape[1]
    q_len = q_rows * n_blocks // n_lab
    label_at = lax.broadcasted_iota(jnp.int32, (q_rows, LANES), 0) // q_len
    column = lax.broadcasted_iota(jnp.int32, (q_rows, LANES), 1)
    for b in range(n_blocks):
        members[b] = jnp.where(column == label_at + b * (n_lab // n_blocks), 1.0, 0.0).astype(
            jnp.bfloat16
        )
    base[...] += acc[z]

    @pl.when(jnp.logical_or(z == 0, z == n_exp - 1))
    def _():
        owner = n_exp - 1 - z
        comb_copy(1, owner).wait_recv()
        scales = [scale_of(owner, e) for e in range(2)]
        for h in range(PIECES):
            tok_copy(1, owner, h).wait_recv()
            if h < PIECES - 1:

                for j in range(4):
                    term = product(owner, j, h * piece, piece)
                    part_act[j] = term if h == 0 else part_act[j] + term
        total = None
        for e in range(2):
            term = None
            for c_at in range(2):
                j = 2 * e + c_at
                act = part_act[j] + product(owner, j, width - piece, piece)
                term = after(act, j) if term is None else term + after(act, j)
            total = term * scales[e] if total is None else total + term * scales[e]
        acc[owner] = total
        ret_copy(owner).start()

    loads[7].wait()
    q_in = remote(queries, q_all.at[1 - x], q_ss, q_rs, {"query": 1 - x})
    q_in.wait_recv()

    for dist in range(1, n_exp):
        for side in (-1, 1):
            src = z + side * dist
            inside = (src >= 0) if side < 0 else (src < n_exp)

            @pl.when(inside)
            def _(src=jnp.clip(src, 0, n_exp - 1)):
                ret_wait(src)
                base[...] += ret[src]

    projected = base[...]
    norm = jnp.sqrt(jnp.sum(projected * projected, axis=-1, keepdims=True) + 1e-06)
    scaled = projected / norm
    token_at = lax.broadcasted_iota(jnp.int32, (PLEN, out_width), 0)
    live = []
    for p in range(n_pass):
        block = scaled[p * PLEN : (p + 1) * PLEN]
        live.append(jnp.where(token_at < plens[p], block, block[0:1]))
    embedding = jnp.concatenate(live, axis=0).astype(jnp.bfloat16)
    total = jnp.zeros((3 * 8, LANES), jnp.float32)
    for b in range(n_blocks):
        raw = lax.dot_general(
            embedding, q_all[b], (((1,), (1,)), ((), ())), preferred_element_type=jnp.float32
        )
        best = [
            jnp.max(raw[p * PLEN : (p + 1) * PLEN], axis=0, keepdims=True) for p in range(n_pass)
        ]
        best = jnp.concatenate(best + [jnp.zeros((8 - n_pass, q_rows), jnp.float32)], axis=0)
        first = best.astype(jnp.bfloat16).astype(jnp.float32)
        second = (best - first).astype(jnp.bfloat16).astype(jnp.float32)
        third = best - first - second
        parts = jnp.concatenate([first, second, third], axis=0).astype(jnp.bfloat16)
        total += jnp.dot(parts, members[b], preferred_element_type=jnp.float32)
    summed = total[0:8] + total[8:16] + total[16:24]
    out[...] = summed[:n_pass, :n_lab]

    for owner in range(n_exp):
        pl.when(jnp.logical_and(z + 1 < n_exp, owner <= z))(
            lambda owner=owner: comb_copy(1, owner).wait_send()
        )
        pl.when(jnp.logical_and(z > 0, owner >= z))(
            lambda owner=owner: comb_copy(-1, owner).wait_send()
        )
    for h in range(PIECES):
        for owner in range(n_exp):
            @pl.when(jnp.logical_and(z + 1 < n_exp, owner <= z))
            def _(owner=owner, h=h):
                tok_copy(1, owner, h).wait_send()

            @pl.when(jnp.logical_and(z > 0, owner >= z))
            def _(owner=owner, h=h):
                tok_copy(-1, owner, h).wait_send()

    for owner in range(n_exp):
        @pl.when(owner != z)
        def _(owner=owner):
            ret_copy(owner).wait_send()

    for k in range(W_PIECES):
        wx_copy(k).wait_send()
        wy_copy(k).wait_send()
        wd_copy(0, k).wait_send()
        wd_copy(1, k).wait_send()
    own_copy.wait_send()
    for copy in v_copies:
        copy.wait_send()
    q_copy.wait_send()


def dense_on_device(
    n_exp,
    tokens,
    route_ids,
    gate_values,
    passage_lengths,
    gate_weight,
    up_weight,
    down_weight,
    proj_weight,
    queries,
):
    rows, width = tokens.shape
    units = gate_weight.shape[2]
    out_width = proj_weight.shape[1]
    queries2 = queries.reshape(-1, queries.shape[-1])
    n_experts = n_exp * 2
    v_rows = (units // LANES + 1) * LANES
    any_spec = pl.BlockSpec(memory_space=pl.ANY)
    vmem_spec = pl.BlockSpec(memory_space=pltpu.VMEM)
    dma = pltpu.SemaphoreType.DMA
    bf16, f32 = jnp.bfloat16, jnp.float32
    return pl.pallas_call(
        functools.partial(dense_kernel, n_exp),
        out_shape=jax.ShapeDtypeStruct((passage_lengths.shape[0], queries.shape[0] * 2), f32),
        in_specs=[any_spec] * 6 + [vmem_spec] * 2 + [pl.BlockSpec(memory_space=pltpu.SMEM)],
        out_specs=vmem_spec,
        scratch_shapes=[
            pltpu.VMEM((n_exp, rows, width), bf16),
            pltpu.VMEM((units, width), bf16),
            pltpu.VMEM((width, out_width), bf16),
            pltpu.VMEM((4, 2 * units, width), bf16),
            pltpu.VMEM((4, v_rows, 2 * out_width), bf16),
            pltpu.VMEM((2,) + queries2.shape, bf16),
            pltpu.VMEM((n_exp, n_experts, rows), f32),
            pltpu.VMEM((n_exp, rows, out_width), f32),
            pltpu.VMEM((n_exp, rows, out_width), f32),
            pltpu.VMEM((rows, out_width), f32),
            pltpu.VMEM((4, rows, 2 * units), f32),
            pltpu.VMEM((2, queries2.shape[0], LANES), bf16),
            dma((8,)),
            dma((2, n_exp, PIECES)),
            dma((n_exp, PIECES)),
            dma((2, n_exp)),
            dma((n_exp,)),
            dma,
            dma,
            dma((W_PIECES,)),
            dma((W_PIECES,)),
            dma((W_PIECES,)),
            dma((W_PIECES,)),
            dma((2, W_PIECES)),
            dma((2, W_PIECES)),
            dma((3,)),
            dma((3,)),
            dma,
            dma,
            dma((n_exp,)),
            dma((n_exp,)),
        ],
        compiler_params=pltpu.CompilerParams(collective_id=0, has_side_effects=True),
    )(
        tokens,
        gate_weight[0].T,
        up_weight[0].T,
        down_weight[0].T,
        proj_weight,
        queries2,
        route_ids.T,
        gate_values.T,
        passage_lengths,
    )


def dense_fits(mesh_shape, rows, units, top):
    experts = mesh_shape["expert"] * mesh_shape["query"]
    pairs = all(mesh_shape[a] == 2 for a in ("group", "query", "dp"))
    capacity = max(2, 2 * rows * top // experts)
    return pairs and mesh_shape["expert"] > 2 and capacity >= rows and units % LANES == LANES // 2


def passage_scores(embedding, live_mask, block_queries):
    query_rows = block_queries.reshape(-1, block_queries.shape[-1])
    raw_scores = jnp.dot(embedding, query_rows.T, preferred_element_type=jnp.float32)
    raw_scores = jnp.where(live_mask[:, None], raw_scores, -jnp.inf)
    best_match = jnp.max(raw_scores.reshape(-1, PLEN, raw_scores.shape[-1]), axis=1)
    return jnp.sum(best_match.reshape(best_match.shape[0], -1, block_queries.shape[1]), axis=-1)


def on_device(
    tokens,
    route_ids,
    gate_values,
    passage_lengths,
    gate_weight,
    up_weight,
    down_weight,
    proj_weight,
    queries,
):
    tok_rows, model_width = tokens.shape
    top_count = route_ids.shape[1]
    experts = lax.axis_size("expert") * lax.axis_size("query")
    capacity = max(2, 2 * tok_rows * top_count // experts)
    assignments = tok_rows * top_count
    flat_routes = route_ids.reshape(-1)
    one_hot = (flat_routes[:, None] == jnp.arange(experts, dtype=jnp.int32)[None, :]).astype(
        jnp.int32
    )
    earlier = jnp.cumsum(one_hot, axis=0) - one_hot
    slot_index = jnp.sum(earlier * one_hot, axis=1)
    slot_target = flat_routes * capacity + slot_index
    slot_owner = (
        jnp.full((experts * capacity,), assignments, jnp.int32)
        .at[slot_target]
        .set(jnp.arange(assignments, dtype=jnp.int32))
    )
    padded = jnp.concatenate([tokens, jnp.zeros((1, model_width), tokens.dtype)], axis=0)
    source_row = jnp.where(slot_owner < assignments, slot_owner // top_count, tok_rows)
    outgoing = padded[source_row].reshape(experts, capacity, model_width)
    arrived = lax.all_to_all(outgoing, ("expert", "query"), split_axis=0, concat_axis=0, tiled=True)
    expert_rows = arrived.reshape(experts * capacity, model_width)
    gate_act = jnp.dot(
        expert_rows,
        lax.all_gather(gate_weight[0], "dp", axis=1, tiled=True),
        preferred_element_type=jnp.float32,
    )
    up_act = jnp.dot(
        expert_rows,
        lax.all_gather(up_weight[0], "dp", axis=1, tiled=True),
        preferred_element_type=jnp.float32,
    )
    hidden = (jax.nn.silu(gate_act) * up_act).astype(jnp.bfloat16)
    accumulated = lax.dot_general(
        hidden,
        lax.all_gather(down_weight[0], "dp", axis=1, tiled=True),
        (((1,), (1,)), ((), ())),
        preferred_element_type=jnp.float32,
    )
    results = accumulated.astype(jnp.bfloat16)
    weights = gate_values.reshape(assignments, 1)
    folded = jnp.dot(results, proj_weight, preferred_element_type=jnp.float32)
    returned_rows = lax.all_to_all(
        folded.reshape(experts, capacity, folded.shape[-1]),
        ("expert", "query"),
        split_axis=0,
        concat_axis=0,
        tiled=True,
    )
    picked = returned_rows.reshape(experts * capacity, folded.shape[-1])[slot_target]
    projected = jnp.dot(tokens, proj_weight, preferred_element_type=jnp.float32) + jnp.sum(
        (picked * weights).reshape(tok_rows, top_count, folded.shape[-1]), axis=1
    )
    lengths_norm = jnp.sqrt(jnp.sum(projected * projected, axis=-1, keepdims=True) + 1e-06)
    embedding = (projected / lengths_norm).astype(jnp.bfloat16)
    position = jnp.arange(tok_rows, dtype=jnp.int32) % PLEN
    live_mask = position < jnp.repeat(passage_lengths, PLEN)
    return passage_scores(
        embedding, live_mask, lax.all_gather(queries, "query", axis=0, tiled=True)
    )


def solution(mesh):
    in_specs = (
        P(("group", "expert", "query", "dp"), None),
        P(("group", "expert", "query", "dp"), None),
        P(("group", "expert", "query", "dp"), None),
        P(("group", "expert", "query", "dp")),
        P(("expert", "query"), None, "dp"),
        P(("expert", "query"), None, "dp"),
        P(("expert", "query"), None, "dp"),
        P(),
        P(("group", "query"), None, None),
    )
    out_specs = P(("group", "expert", "query", "dp"), None)
    sizes = dict(mesh.shape)

    def run(tokens, route_ids, *rest):
        units = rest[2].shape[2]
        if dense_fits(sizes, tokens.shape[0], units, route_ids.shape[1]):
            return dense_on_device(sizes["expert"], tokens, route_ids, *rest)
        return on_device(tokens, route_ids, *rest)

    return jax.shard_map(
        run, mesh=mesh, in_specs=in_specs, out_specs=out_specs, check_vma=False
    )
```
